32 devices in a mesh: dp: 8 (over z, x), seq: 4 (over y, core).
Axes of the slice: x: 2, y: 2, z: 4, core: 2. Of those that a mesh axis runs over, the one named last changes fastest.
Arguments:
- residual_tiles: bfloat16 [8, 1024, 1024], P('dp', 'seq'), may hold values from -16 to 16
- picture_label_tile: int32 [8, 1024], P('dp', 'seq'), may hold values from 0 to 11, never falling along the last dimension, each value on 1 to 512 neighbouring positions
- prenorm_multiplier: float32 [1024], replicated, may hold values from 0.5 to 1.5
- triple_projector: bfloat16 [1024, 3072], P('dp'), may hold values from -0.25 to 0.25
- logit_scaling: float32 [16], replicated, may hold values from 0.3 to 30
- final_projector: bfloat16 [1024, 1024], P('dp'), may hold values from -0.1875 to 0.1875
- binarizer_projector: bfloat16 [1024, 18], replicated, may hold values from -0.1875 to 0.1875
- binarizer_offset: float32 [18], replicated, may hold values from -1 to 1
Outputs:
- mixed: bfloat16 [8, 1024, 1024], P('dp', 'seq')
- bit_codes: float32 [8, 18, 1024], P('dp', None, 'seq')
- code_entropy: float32 [18], replicated
The draws below stay inside these ranges and needn't reach their ends.
Inputs may be any that keep to these rules, and one draw needn't show every extreme that they name: `picture_label_tile`: in each pack image numbers never fall, every image number of 0 to 11 occurs, and an image has at most 512 patches.
All inputs are finite; a program needn't handle non-finite values.
Results may differ from the reference program's by a relative error of at most 0.0053.
The reference program's roundings to bfloat16 on the way count: a program that leaves them out, or rounds other values in their place, can miss the bound.
Values may be sent and summed in bfloat16 or wider, within the bound.
A program may use at most 64 MiB of HBM per device.

```python
import math
import jax
import jax.numpy as jnp
import numpy as np
from jax import lax

D = 1024
HEADS = 16
CHANNEL_COUNT = 64
BITS = 18
IMAGES = 12
SEQ = 1024
PACKS = 8


def draw_residual_tiles(key, part):
    first_key, second_key = jax.random.split(key, 2)
    pack_place = jnp.arange(PACKS, dtype=jnp.float32) / max(PACKS - 1, 1)
    token_place = jnp.arange(SEQ, dtype=jnp.float32) / max(SEQ - 1, 1)
    trend = jnp.exp(jnp.log(3.0) * pack_place)[:, None] * jnp.exp(jnp.log(2.0) * token_place)[None, :]
    rough = jnp.exp(jax.random.uniform(first_key, (PACKS, SEQ), minval=jnp.log(0.4), maxval=jnp.log(1.6)))
    base = jax.random.normal(second_key, (PACKS, SEQ, D))
    values = base * (trend * rough)[:, :, None] * 0.5
    return jnp.clip(values, -16.0, 16.0).astype(jnp.bfloat16)


def draw_triple_projector(key, part):
    first_key = jax.random.fold_in(key, 0)
    spread = D ** (-0.5)
    base = jax.random.normal(first_key, (D, 3, D)) * spread
    return jnp.clip(base.reshape(D, 3 * D), -0.25, 0.25).astype(jnp.bfloat16)


def draw_logit_scaling(key, part):
    first_key = jax.random.fold_in(key, 0)
    values = jnp.exp(jax.random.uniform(first_key, (HEADS,), minval=jnp.log(0.3), maxval=jnp.log(3.0)))
    return values.astype(jnp.float32)


def steps_of(key, extent, shards, smallest, largest):
    level, own = 1.0, jax.random.fold_in(key, 6)
    for dim, shards_of in shards:
        draws = jnp.exp(jax.random.uniform(jax.random.fold_in(own, dim), (shards_of,), jnp.float32, smallest / len(shards), largest / len(shards)))
        level = level * jnp.repeat(draws, extent[dim] // shards_of).reshape([-1 if axis == dim else 1 for axis in range(len(extent))])
    return level


def profile(amount, total, reach, lean):
    portions = [(1 << 20) // math.isqrt(rank ** lean) + 1 for rank in range(2, amount + 1)]
    surplus, holding = total - reach - (amount - 1), [1] * (amount - 1)
    while surplus > 0:
        free = [i for i in range(amount - 1) if holding[i] < reach]
        whole, budget = sum([portions[i] for i in free]), surplus
        for i in free:
            more = min(reach - holding[i], max(1, budget * portions[i] // whole), surplus)
            holding[i] = holding[i] + more
            surplus = surplus - more
    return np.array([reach] + holding)


def uneven(rng, number_of, total, limit, slope):
    if number_of == 2:
        one = jax.random.randint(rng, (), max(1, total - limit), min(limit, total - 1) + 1)
        return jnp.stack([one, total - one])
    sizes = jnp.asarray(profile(number_of, total, limit, slope), jnp.int32)
    twos = (number_of - 1) // 2
    donor, taker = sizes[1:1 + 2 * twos:2], sizes[2:2 + 2 * twos:2]
    margin = jnp.minimum(donor - 1, limit - taker)
    shifted = jax.random.randint(jax.random.fold_in(rng, 1), (twos,), 0, 1 << 20) % (margin + 1)
    sizes = sizes.at[1:1 + 2 * twos:2].set(donor - shifted).at[2:2 + 2 * twos:2].set(taker + shifted)
    return sizes[jax.random.permutation(jax.random.fold_in(rng, 2), number_of)]


def gaussian(stream_key, extent, scale, reach, cuts=(), kind=jnp.bfloat16):
    factor_of = steps_of(stream_key, extent, cuts, -0.22, 0.18) if cuts else 1.0
    result = jax.random.normal(stream_key, extent, jnp.float32) * scale * factor_of
    return jnp.minimum(jnp.maximum(result, -reach), reach).astype(kind)


def setup_inputs(seed: int = 0) -> dict:
    keys = jax.random.split(jax.random.key(seed), 9)
    return {
        "residual_tiles": draw_residual_tiles(jax.random.fold_in(keys[8], 71), 0),
        "picture_label_tile": jax.vmap(lambda own: jnp.searchsorted(jnp.cumsum(uneven(own, IMAGES, SEQ, SEQ // 2, 2)), jnp.arange(SEQ), side="right"))(jax.random.split(keys[1], PACKS)).reshape((PACKS, SEQ)).astype(jnp.int32),
        "prenorm_multiplier": jnp.clip(1.0 + 0.1 * jax.random.normal(keys[2], (D,), jnp.float32), 0.5, 1.5),
        "triple_projector": draw_triple_projector(jax.random.fold_in(keys[8], 71), 0),
        "logit_scaling": draw_logit_scaling(jax.random.fold_in(keys[8], 71), 0),
        "final_projector": gaussian(keys[5], (D, D), D ** -0.5, 0.1875, ((0, 8),)),
        "binarizer_projector": gaussian(keys[6], (D, BITS), D ** -0.5, 0.1875),
        "binarizer_offset": jnp.clip(jax.random.uniform(keys[7], (BITS,), jnp.float32, -1.0, 1.0), -1.0, 1.0),
    }


epsilon = 1e-06

def rms_scale(values):
    return lax.rsqrt(lax.optimization_barrier(jnp.mean(values * values, axis=-1, keepdims=True)) + epsilon)

def split_subspaces(combined_subspaces, scales, channel_extent):
    token_count = combined_subspaces.shape[0]
    pieces = combined_subspaces.reshape(token_count, 3, scales.shape[0], channel_extent).astype(jnp.float32)
    asking_tensor = pieces[:, 0] * rms_scale(pieces[:, 0]) * (scales[:, None] / math.sqrt(channel_extent))
    rescaled_lookups = pieces[:, 1] * rms_scale(pieces[:, 1])
    return (asking_tensor.astype(jnp.bfloat16), rescaled_lookups.astype(jnp.bfloat16), pieces[:, 2].astype(jnp.bfloat16))

def bundled_mixing_block(bundled_tokens, picture_label_column, prenorm_multiplier, triple_projector, logit_scaling, final_projector, binarizer_projector, binarizer_offset):
    wide_pack = bundled_tokens.astype(jnp.float32)
    normed = (wide_pack * rms_scale(wide_pack) * prenorm_multiplier).astype(jnp.bfloat16)
    combined_subspaces = jnp.dot(normed, triple_projector, preferred_element_type=jnp.float32).astype(jnp.bfloat16)
    asking_tensor, rescaled_lookups, surviving_contents = split_subspaces(combined_subspaces, logit_scaling, CHANNEL_COUNT)
    same_image = picture_label_column[:, None] == picture_label_column[None, :]

    def one_head(contraction_operands):
        query_head, key_head, value_head = contraction_operands
        scores = jnp.dot(query_head, key_head.T, preferred_element_type=jnp.float32)
        masked = jnp.where(same_image, scores, -1e+30)
        highest = lax.optimization_barrier(jnp.max(masked, axis=-1, keepdims=True))
        probs = jnp.where(same_image, jnp.exp(scores - highest), 0.0)
        weights = probs.astype(jnp.bfloat16)
        summed = jnp.dot(weights, value_head, preferred_element_type=jnp.float32)
        return summed / lax.optimization_barrier(jnp.sum(probs, axis=-1, keepdims=True))
    attended = lax.map(one_head, (jnp.swapaxes(asking_tensor, 0, 1), jnp.swapaxes(rescaled_lookups, 0, 1), jnp.swapaxes(surviving_contents, 0, 1)))
    attention = jnp.swapaxes(attended, 0, 1).reshape(SEQ, D).astype(jnp.bfloat16)
    hidden_state = wide_pack + jnp.dot(attention, final_projector, preferred_element_type=jnp.float32)
    mixed = hidden_state.astype(jnp.bfloat16)
    logits = jnp.dot(mixed, binarizer_projector, preferred_element_type=jnp.float32) + binarizer_offset
    return (mixed, jax.nn.sigmoid(4.0 * logits))

def reference(residual_tiles, picture_label_tile, prenorm_multiplier, triple_projector, logit_scaling, final_projector, binarizer_projector, binarizer_offset):

    def one_pack(contraction_operands):
        return bundled_mixing_block(contraction_operands[0], contraction_operands[1], prenorm_multiplier, triple_projector, logit_scaling, final_projector, binarizer_projector, binarizer_offset)
    mixed, bit_probs = lax.map(one_pack, (residual_tiles, picture_label_tile))
    marginal = lax.optimization_barrier(jnp.sum(bit_probs, axis=(0, 1))) / (PACKS * SEQ)
    code_entropy = -(marginal * jnp.log(marginal) + (1.0 - marginal) * jnp.log(1.0 - marginal))
    bit_codes = jnp.swapaxes(bit_probs - marginal, 1, 2)
    return (mixed, bit_codes, code_entropy)
```

```python
import functools
import math

import jax
import jax.numpy as jnp
from jax import lax
from jax.experimental import pallas as pl
from jax.experimental.pallas import tpu as pltpu
from jax.sharding import PartitionSpec as P

EPS = 1e-06
MESH = pl.DeviceIdType.MESH
NEG = -1e30


def layer_kernel(
    cfg,
    x_ref,
    ids_ref,
    gain_ref,
    w_ref,
    scale_ref,
    wo_ref,
    bits_ref,
    off_ref,
    mixed_ref,
    codes_ref,
    ent_ref,
    wg,
    wog,
    xg,
    idg,
    idcol,
    normed,
    acc,
    qs,
    ks,
    vs,
    ao,
    ag,
    part1,
    part2,
    local_sem,
    wz_s,
    wz_r,
    wx_s,
    wx_r,
    oz_s,
    oz_r,
    ox_s,
    ox_r,
    oy_s,
    oy_r,
    oc_s,
    oc_r,
    xy_s,
    xy_r,
    xc_s,
    xc_r,
    id_s,
    id_r,
    at_s,
    at_r,
    p1_s,
    p1_r,
    p2_s,
    p2_r,
):
    nz, nx, ny, nc = cfg["nz"], cfg["nx"], cfg["ny"], cfg["nc"]
    n = ny * nc
    ndp = nz * nx
    heads, channel = cfg["heads"], cfg["channel"]
    rows, width = x_ref.shape
    shard = w_ref.shape[0]
    chunk = nx * shard
    cols = width // n
    seq_len = rows * n
    bits = bits_ref.shape[0]
    dp = lax.axis_index("dp")
    me = lax.axis_index("seq")
    z = dp // nx
    x = dp % nx
    y = me // nc
    core = me % nc

    def dp_at(zz, xx):
        return zz * nx + xx

    def seq_at(yy, cc):
        return yy * nc + cc

    def remote(src, dst, ss, rs, d, s):
        return pltpu.make_async_remote_copy(
            src_ref=src, dst_ref=dst, send_sem=ss, recv_sem=rs, device_id=(d, s), device_id_type=MESH
        )

    def w_slot(zz, xx):
        return wg.at[zz, pl.ds(pl.multiple_of(xx * shard, shard), shard), :]

    def o_slot(zz, xx):
        return wog.at[me, pl.ds(pl.multiple_of(dp_at(zz, xx) * shard, shard), shard), :]

    own = []
    for part in range(3):
        own.append(
            pltpu.make_async_copy(
                w_ref.at[:, pl.ds(pl.multiple_of(part * width + me * cols, 128), cols)],
                wg.at[
                    z,
                    pl.ds(pl.multiple_of(x * shard, shard), shard),
                    pl.ds(part * cols, cols),
                ],
                local_sem.at[part],
            )
        )
    own.append(pltpu.make_async_copy(x_ref, xg.at[me], local_sem.at[3]))
    own.append(pltpu.make_async_copy(ids_ref, idg.at[me], local_sem.at[4]))
    own.append(
        pltpu.make_async_copy(
            wo_ref.at[:, pl.ds(pl.multiple_of(me * cols, 128), cols)], o_slot(z, x), local_sem.at[5]
        )
    )
    for c in own:
        c.start()

    barrier = pltpu.get_barrier_semaphore()

    def greet_seq(i, _):
        pl.semaphore_signal(
            barrier, inc=1, device_id=(dp, (me + i) % n), device_id_type=MESH
        )
        return 0

    def greet_dp(i, _):
        pl.semaphore_signal(
            barrier, inc=1, device_id=((dp + i) % ndp, me), device_id_type=MESH
        )
        return 0

    lax.fori_loop(1, n, greet_seq, 0)
    lax.fori_loop(1, ndp, greet_dp, 0)
    pl.semaphore_wait(barrier, n - 1 + ndp - 1)

    sends = []

    def go(c):
        c.start()
        sends.append(c)

    own[0].wait()
    own[1].wait()
    own[2].wait()
    for i in range(1, nz):
        go(remote(w_slot(z, x), w_slot(z, x), wz_s.at[i], wz_r.at[i], dp_at((z + i) % nz, x), me))
    for k in range(1, nx):
        go(remote(w_slot(z, x), w_slot(z, x), wx_s.at[0, k], wx_r.at[0, k], dp_at(z, (x + k) % nx), me))
    own[3].wait()
    for i in range(1, ny):
        go(remote(xg.at[me], xg.at[me], xy_s.at[i], xy_r.at[i], dp, seq_at((y + i) % ny, core)))
    for k in range(1, nc):
        go(remote(xg.at[me], xg.at[me], xc_s.at[0, k], xc_r.at[0, k], dp, seq_at(y, (core + k) % nc)))
    own[4].wait()
    for i in range(1, n):
        go(remote(idg.at[me], idg.at[me], id_s.at[i], id_r.at[i], dp, (me + i) % n))
    own[5].wait()
    for i in range(1, nz):
        go(remote(o_slot(z, x), o_slot(z, x), oz_s.at[i], oz_r.at[i], dp_at((z + i) % nz, x), me))
    for k in range(1, nx):
        go(remote(o_slot(z, x), o_slot(z, x), ox_s.at[0, k], ox_r.at[0, k], dp_at(z, (x + k) % nx), me))

    gain = gain_ref[...]

    def norm_rows(member):
        base = pl.multiple_of(member * rows, rows)

        def body(b, _):
            r0 = pl.multiple_of(b * 64, 64)
            wide = xg[member, pl.ds(r0, 64), :].astype(jnp.float32)
            ms = jnp.mean(wide * wide, axis=-1, keepdims=True)
            out = (wide * lax.rsqrt(ms + EPS) * gain).astype(jnp.bfloat16)
            for g in range(nz):
                normed[g, pl.ds(base + r0, 64), :] = out[:, g * chunk : (g + 1) * chunk]
            return 0

        lax.fori_loop(0, rows // 64, body, 0)

    def arrive(slot, sem):
        remote(slot, slot, sem, sem, dp, me).wait_recv()

    def w_forward(i):
        zz = (z - i + nz) % nz
        arrive(w_slot(zz, x), wz_r.at[i])
        for k in range(1, nx):
            go(remote(w_slot(zz, x), w_slot(zz, x), wx_s.at[i, k], wx_r.at[i, k], dp_at(z, (x + k) % nx), me))

    norm_rows(me)
    for k in range(1, nc):
        other = seq_at(y, (core - k + nc) % nc)
        arrive(xg.at[other], xc_r.at[0, k])
        norm_rows(other)
    for i in range(1, nz - 1):
        w_forward(i)
    for i in range(1, ny):
        yy = (y - i + ny) % ny
        source = seq_at(yy, core)
        arrive(xg.at[source], xy_r.at[i])
        for k in range(1, nc):
            go(remote(xg.at[source], xg.at[source], xc_s.at[i, k], xc_r.at[i, k], dp, seq_at(y, (core + k) % nc)))
        norm_rows(source)
    for i in range(1, ny):
        yy = (y - i + ny) % ny
        for k in range(1, nc):
            other = seq_at(yy, (core - k + nc) % nc)
            arrive(xg.at[other], xc_r.at[i, k])
            norm_rows(other)

    for i in range(1, n):
        arrive(idg.at[(me - i + n) % n], id_r.at[i])
    for m in range(n):
        line = jnp.broadcast_to(idg[m].astype(jnp.float32), (128, rows))
        idcol[pl.ds(m * rows, rows), :] = jnp.transpose(line)
    id_row = jnp.concatenate([idg[m] for m in range(n)], axis=1).astype(jnp.float32)

    row_block = 256
    blocks = seq_len // row_block

    def project(i, first):
        zz = (z - i + nz) % nz
        for k in range(1, nx):
            arrive(w_slot(zz, (x - k + nx) % nx), wx_r.at[i, k])

        def body(b, _):
            r = pl.ds(pl.multiple_of(b * row_block, row_block), row_block)
            prod = jnp.dot(normed[zz, r, :], wg[zz], preferred_element_type=jnp.float32)
            if first:
                acc[r, :] = prod
            else:
                acc[r, :] = acc[r, :] + prod
            return 0

        lax.fori_loop(0, blocks, body, 0)

    for i in range(nz):
        if i == max(0, nz - 2):
            if nz > 1:
                w_forward(nz - 1)
        project(i, i == 0)

    def group_of(shape, dim):
        return lax.div(lax.broadcasted_iota(jnp.int32, shape, dim), jnp.int32(channel))

    same_head = (group_of((cols, cols), 0) == group_of((cols, cols), 1)).astype(jnp.float32)
    same_head = same_head.astype(jnp.bfloat16)
    scale_row = scale_ref[:, pl.ds(pl.multiple_of(me * cols, 128), cols)] / math.sqrt(channel)

    def head_scale(values):
        square = values * values
        high = square.astype(jnp.bfloat16)
        low = (square - high.astype(jnp.float32)).astype(jnp.bfloat16)
        total = jnp.dot(high, same_head, preferred_element_type=jnp.float32) + jnp.dot(
            low, same_head, preferred_element_type=jnp.float32
        )
        return lax.rsqrt(total / channel + EPS)

    def split(b, _):
        r = pl.ds(pl.multiple_of(b * row_block, row_block), row_block)
        joined = acc[r, :].astype(jnp.bfloat16)
        q = joined[:, :cols].astype(jnp.float32)
        k = joined[:, cols : 2 * cols].astype(jnp.float32)
        qs[r, :] = (q * head_scale(q) * scale_row).astype(jnp.bfloat16)
        ks[r, :] = (k * head_scale(k)).astype(jnp.bfloat16)
        vs[r, :] = joined[:, 2 * cols :]
        return 0

    lax.fori_loop(0, blocks, split, 0)

    for i in range(1, nz):
        zz = (z - i + nz) % nz
        arrive(o_slot(zz, x), oz_r.at[i])
        for k in range(1, nx):
            go(remote(o_slot(zz, x), o_slot(zz, x), ox_s.at[i, k], ox_r.at[i, k], dp_at(z, (x + k) % nx), me))

    q_block = cfg["q_block"]
    lane_head = group_of((q_block, cols), 1)

    def stage_target(t, sign):
        dy = (t // nc + 1) % ny
        dc = (t + 1) % nc
        if sign > 0:
            return seq_at((y + dy) % ny, (core + dc) % nc)
        return seq_at((y - dy + ny) % ny, (core - dc + nc) % nc)

    def a2a(t):
        j = stage_target(t, 1)
        return remote(ao.at[j], ag.at[me], at_s.at[t], at_r.at[t], dp, j)

    oy = [
        remote(wog.at[me], wog.at[me], oy_s.at[i], oy_r.at[i], dp, seq_at((y + i) % ny, core))
        for i in range(1, ny)
    ]
    oc = [
        remote(wog.at[me], wog.at[me], oc_s.at[0, k], oc_r.at[0, k], dp, seq_at(y, (core + k) % nc))
        for k in range(1, nc)
    ]
    oc_late = []
    for i in range(1, ny):
        source = seq_at((y - i + ny) % ny, core)
        for k in range(1, nc):
            oc_late.append(
                remote(wog.at[source], wog.at[source], oc_s.at[i, k], oc_r.at[i, k], dp, seq_at(y, (core + k) % nc))
            )

    def stage(t, _):
        j = stage_target(t, 1)
        for sub in range(rows // q_block):
            r = pl.ds(pl.multiple_of(j * rows + sub * q_block, q_block), q_block)
            bias = jnp.where(idcol[r, :][:, :1] == id_row, 0.0, NEG)
            qb = qs[r, :]
            out = jnp.zeros((q_block, cols), jnp.float32)
            for h in range(heads):
                mine = lane_head == h
                qh = jnp.where(mine, qb, jnp.zeros_like(qb))
                s = lax.dot_general(
                    qh, ks[...], (((1,), (1,)), ((), ())), preferred_element_type=jnp.float32
                )
                s = s + bias
                p = jnp.exp(s - jnp.max(s, axis=-1, keepdims=True))
                total = jnp.sum(p, axis=-1, keepdims=True)
                o = jnp.dot(p.astype(jnp.bfloat16), vs[...], preferred_element_type=jnp.float32)
                out = jnp.where(mine, o / total, out)
            ao[j, pl.ds(sub * q_block, q_block), :] = out.astype(jnp.bfloat16)

        @pl.when(t < n - 1)
        def _():
            a2a(t).start()

        @pl.when(t == 0)
        def _():
            for i in range(nz):
                zz = (z - i + nz) % nz
                for k in range(1, nx):
                    arrive(o_slot(zz, (x - k + nx) % nx), ox_r.at[i, k])
            for c in oy + oc:
                c.start()

        @pl.when(t == n - 2)
        def _():
            for i in range(1, ny):
                arrive(wog.at[seq_at((y - i + ny) % ny, core)], oy_r.at[i])
            for c in oc_late:
                c.start()

        return 0

    lax.fori_loop(0, n, stage, 0)
    sends.extend(oy + oc + oc_late)

    for i in range(ny):
        for k in range(1, nc):
            arrive(wog.at[seq_at((y - i + ny) % ny, (core - k + nc) % nc)], oc_r.at[i, k])
    for t in range(n - 1):
        arrive(ag.at[stage_target(t, -1)], at_r.at[t])
    ag[me] = ao[me]

    attention = jnp.concatenate([ag[m] for m in range(n)], axis=1)
    for g in range(n):
        lanes = slice(g * cols, (g + 1) * cols)
        prod = jnp.dot(attention, wog[g], preferred_element_type=jnp.float32)
        mixed_ref[:, lanes] = (xg[me, :, lanes].astype(jnp.float32) + prod).astype(jnp.bfloat16)

    logits = lax.dot_general(
        bits_ref[...], mixed_ref[...], (((1,), (1,)), ((), ())), preferred_element_type=jnp.float32
    )
    probs = jax.nn.sigmoid(4.0 * (logits + off_ref[...]))
    part1[me, :, :] = jnp.broadcast_to(jnp.sum(probs, axis=1, keepdims=True), (bits, 128))
    for i in range(1, n):
        go(remote(part1.at[me], part1.at[me], p1_s.at[i], p1_r.at[i], dp, (me + i) % n))
    for i in range(1, n):
        arrive(part1.at[(me - i + n) % n], p1_r.at[i])
    pack = part1[0]
    for m in range(1, n):
        pack = pack + part1[m]
    part2[dp, :, :] = pack
    for i in range(1, ndp):
        go(remote(part2.at[dp], part2.at[dp], p2_s.at[i], p2_r.at[i], (dp + i) % ndp, me))
    for i in range(1, ndp):
        arrive(part2.at[(dp - i + ndp) % ndp], p2_r.at[i])
    total = part2[0]
    for m in range(1, ndp):
        total = total + part2[m]
    marginal = total / (seq_len * ndp)
    ent_ref[...] = -(marginal * jnp.log(marginal) + (1.0 - marginal) * jnp.log(1.0 - marginal))
    codes_ref[...] = probs - marginal[:, :1]

    for c in sends:
        c.wait_send()
    for t in range(n - 1):
        a2a(t).wait_send()


def on_device(
    cfg,
    residual_tiles,
    picture_label_tile,
    prenorm_multiplier,
    triple_projector,
    logit_scaling,
    final_projector,
    binarizer_projector,
    binarizer_offset,
):
    nz, nx, ny, nc = cfg["nz"], cfg["nx"], cfg["ny"], cfg["nc"]
    n, ndp = ny * nc, nz * nx
    _, rows, width = residual_tiles.shape
    heads_all = logit_scaling.shape[0]
    bits = binarizer_projector.shape[1]
    cols = width // n
    shard = triple_projector.shape[0]
    seq_len = rows * n
    cfg = dict(cfg, heads=heads_all // n, channel=width // heads_all, q_block=min(256, rows))
    dma = pltpu.SemaphoreType.DMA
    vmem, hbm = pl.BlockSpec(memory_space=pltpu.VMEM), pl.BlockSpec(memory_space=pl.ANY)
    bf16, f32 = jnp.bfloat16, jnp.float32
    mixed, codes, ent = pl.pallas_call(
        functools.partial(layer_kernel, cfg),
        out_shape=(
            jax.ShapeDtypeStruct((rows, width), bf16),
            jax.ShapeDtypeStruct((bits, rows), f32),
            jax.ShapeDtypeStruct((bits, 128), f32),
        ),
        in_specs=[hbm, vmem, vmem, hbm, vmem, hbm, vmem, vmem],
        out_specs=(vmem, vmem, vmem),
        scratch_shapes=[
            pltpu.VMEM((nz, nx * shard, 3 * cols), bf16),
            pltpu.VMEM((n, width, cols), bf16),
            pltpu.VMEM((n, rows, width), bf16),
            pltpu.VMEM((n, 1, rows), jnp.int32),
            pltpu.VMEM((seq_len, 128), f32),
            pltpu.VMEM((nz, seq_len, nx * shard), bf16),
            pltpu.VMEM((seq_len, 3 * cols), f32),
            pltpu.VMEM((seq_len, cols), bf16),
            pltpu.VMEM((seq_len, cols), bf16),
            pltpu.VMEM((seq_len, cols), bf16),
            pltpu.VMEM((n, rows, cols), bf16),
            pltpu.VMEM((n, rows, cols), bf16),
            pltpu.VMEM((n, bits, 128), f32),
            pltpu.VMEM((ndp, bits, 128), f32),
            dma((6,)),
            dma((nz,)),
            dma((nz,)),
            dma((nz, nx)),
            dma((nz, nx)),
            dma((nz,)),
            dma((nz,)),
            dma((nz, nx)),
            dma((nz, nx)),
            dma((ny,)),
            dma((ny,)),
            dma((ny, nc)),
            dma((ny, nc)),
            dma((ny,)),
            dma((ny,)),
            dma((ny, nc)),
            dma((ny, nc)),
            dma((n,)),
            dma((n,)),
            dma((n,)),
            dma((n,)),
            dma((n,)),
            dma((n,)),
            dma((ndp,)),
            dma((ndp,)),
        ],
        compiler_params=pltpu.CompilerParams(
            collective_id=0, has_side_effects=True, vmem_limit_bytes=60 * 1024 * 1024
        ),
        name="layer",
    )(
        residual_tiles[0],
        picture_label_tile,
        prenorm_multiplier[None],
        triple_projector,
        jnp.repeat(logit_scaling, width // heads_all)[None],
        final_projector,
        binarizer_projector.T,
        binarizer_offset[:, None],
    )
    return mixed[None], codes[None], ent[:, 0]


def solution(mesh):
    ndp, n = mesh.shape["dp"], mesh.shape["seq"]
    nx = math.isqrt(ndp // 2)
    if nx < 1 or ndp % nx:
        nx = 1
    nc = 2 if n % 2 == 0 else 1
    cfg = {"nz": ndp // nx, "nx": nx, "ny": n // nc, "nc": nc}
    return jax.shard_map(
        functools.partial(on_device, cfg),
        mesh=mesh,
        in_specs=(
            P("dp", "seq", None),
            P("dp", "seq"),
            P(),
            P("dp", None),
            P(),
            P("dp", None),
            P(),
            P(),
        ),
        out_specs=(P("dp", "seq", None), P("dp", None, "seq"), P()),
        check_vma=False,
    )
```

```python
import functools
import math

import jax
import jax.numpy as jnp
from jax import lax
from jax.experimental import pallas as pl
from jax.experimental.pallas import tpu as pltpu
from jax.sharding import PartitionSpec as P

EPS = 1e-06
MESH = pl.DeviceIdType.MESH
NEG = -1e30


def layer_kernel(
    cfg,
    x_ref,
    ids_ref,
    gain_ref,
    w_ref,
    scale_ref,
    wo_ref,
    bits_ref,
    off_ref,
    mixed_ref,
    codes_ref,
    ent_ref,
    wg,
    wog,
    xg,
    idg,
    idcol,
    normed,
    acc,
    qs,
    ks,
    vs,
    ao,
    ag,
    part1,
    part2,
    local_sem,
    wz_s,
    wz_r,
    wx_s,
    wx_r,
    oz_s,
    oz_r,
    ox_s,
    ox_r,
    oc_s,
    oc_r,
    xy_s,
    xy_r,
    xc_s,
    xc_r,
    id_s,
    id_r,
    at_s,
    at_r,
    p1_s,
    p1_r,
    p2_s,
    p2_r,
):
    nz, nx, ny, nc = cfg["nz"], cfg["nx"], cfg["ny"], cfg["nc"]
    n = ny * nc
    ndp = nz * nx
    heads, channel = cfg["heads"], cfg["channel"]
    rows, width = x_ref.shape
    shard = w_ref.shape[0]
    chunk = nx * shard
    cols = width // n
    seq_len = rows * n
    bits = bits_ref.shape[0]
    dp = lax.axis_index("dp")
    me = lax.axis_index("seq")
    late = cfg["late"]
    z = dp // nx
    x = dp % nx
    y = me // nc
    core = me % nc

    def dp_at(zz, xx):
        return zz * nx + xx

    def seq_at(yy, cc):
        return yy * nc + cc

    def remote(src, dst, ss, rs, d, s):
        return pltpu.make_async_remote_copy(
            src_ref=src, dst_ref=dst, send_sem=ss, recv_sem=rs, device_id=(d, s), device_id_type=MESH
        )

    sends = []

    def go(c):
        c.start()
        sends.append(c)

    def arrive(slot, sem):
        remote(slot, slot, sem, sem, dp, me).wait_recv()

    def w_slot(zz, xx):
        return wg.at[zz, pl.ds(pl.multiple_of(xx * shard, shard), shard), :]

    def o_slot(zz, xx):
        return wog.at[core, pl.ds(pl.multiple_of(dp_at(zz, xx) * shard, shard), shard), :]

    lo = jnp.minimum(z, nz - 1 - z)

    def piece(i):
        near = z - (i + 1) // 2 if i % 2 else z + (i + 1) // 2
        far = jnp.where(z > nz - 1 - z, z - (i - lo), z + (i - lo))
        return jnp.where(i <= 2 * lo, near, far) if i else z

    def first_hops(slot, ss, rs):
        left = remote(slot(z, x), slot(z, x), ss.at[nz], rs.at[z], dp_at(jnp.maximum(z - 1, 0), x), me)
        right = remote(
            slot(z, x), slot(z, x), ss.at[nz + 1], rs.at[z], dp_at(jnp.minimum(z + 1, nz - 1), x), me
        )
        return left, right

    def next_hops(slot, ss, rs, i):
        p = piece(i)
        left = remote(slot(p, x), slot(p, x), ss.at[p], rs.at[p], dp_at(jnp.maximum(z - 1, 0), x), me)
        right = remote(
            slot(p, x), slot(p, x), ss.at[p], rs.at[p], dp_at(jnp.minimum(z + 1, nz - 1), x), me
        )
        return left, right

    line_sends = []

    def line_start(slot, ss, rs, i):
        if nz == 1:
            return
        p = piece(i)
        left, right = next_hops(slot, ss, rs, i) if i else first_hops(slot, ss, rs)
        to_left = jnp.logical_and(p >= z, z > 0)
        to_right = jnp.logical_and(p <= z, z < nz - 1)
        line_sends.append((to_left, left))
        line_sends.append((to_right, right))

        @pl.when(to_left)
        def _():
            left.start()

        @pl.when(to_right)
        def _():
            right.start()

    def across(slot, ss, rs, i):
        p = piece(i)
        for k in range(1, nx):
            go(remote(slot(p, x), slot(p, x), ss.at[p, k], rs.at[p, k], dp_at(z, (x + k) % nx), me))

    def shared(p, xx, k):
        idx = dp_at(p, xx)
        slot = o_slot(p, xx)
        return remote(slot, slot, oc_s.at[idx, k], oc_r.at[idx, k], dp, seq_at(y, (core + k) % nc))

    def share(p, xx):
        for k in range(1, nc):
            shared(p, xx, k).start()

    def w_relay(i):
        p = piece(i)
        arrive(w_slot(p, x), wz_r.at[p])
        line_start(w_slot, wz_s, wz_r, i)
        across(w_slot, wx_s, wx_r, i)

    def o_relay(i):
        p = piece(i)
        arrive(o_slot(p, x), oz_r.at[p])
        line_start(o_slot, oz_s, oz_r, i)
        across(o_slot, ox_s, ox_r, i)
        share(p, x)

    def o_crossed(i):
        p = piece(i)
        for k in range(1, nx):
            xx = (x - k + nx) % nx
            arrive(o_slot(p, xx), ox_r.at[p, k])
            share(p, xx)

    own = []
    for part in range(3):
        own.append(
            pltpu.make_async_copy(
                w_ref.at[:, pl.ds(pl.multiple_of(part * width + me * cols, 128), cols)],
                wg.at[
                    z,
                    pl.ds(pl.multiple_of(x * shard, shard), shard),
                    pl.ds(part * cols, cols),
                ],
                local_sem.at[part],
            )
        )
    own.append(pltpu.make_async_copy(x_ref, xg.at[me], local_sem.at[3]))
    own.append(pltpu.make_async_copy(ids_ref, idg.at[me], local_sem.at[4]))
    own.append(
        pltpu.make_async_copy(
            wo_ref.at[:, pl.ds(pl.multiple_of(core * (width // nc), 128), width // nc)],
            o_slot(z, x),
            local_sem.at[5],
        )
    )
    for c in own:
        c.start()

    barrier = pltpu.get_barrier_semaphore()

    def greet_seq(i, _):
        pl.semaphore_signal(
            barrier, inc=1, device_id=(dp, (me + i) % n), device_id_type=MESH
        )
        return 0

    def greet_dp(i, _):
        pl.semaphore_signal(
            barrier, inc=1, device_id=((dp + i) % ndp, me), device_id_type=MESH
        )
        return 0

    lax.fori_loop(1, n, greet_seq, 0)
    lax.fori_loop(1, ndp, greet_dp, 0)
    pl.semaphore_wait(barrier, n - 1 + ndp - 1)

    own[0].wait()
    own[1].wait()
    own[2].wait()
    line_start(w_slot, wz_s, wz_r, 0)
    across(w_slot, wx_s, wx_r, 0)
    own[3].wait()
    for i in range(1, ny):
        go(remote(xg.at[me], xg.at[me], xy_s.at[i], xy_r.at[i], dp, seq_at((y + i) % ny, core)))
    for k in range(1, nc):
        go(remote(xg.at[me], xg.at[me], xc_s.at[0, k], xc_r.at[0, k], dp, seq_at(y, (core + k) % nc)))
    own[4].wait()
    for i in range(1, n):
        go(remote(idg.at[me], idg.at[me], id_s.at[i], id_r.at[i], dp, (me + i) % n))
    own[5].wait()
    if not late:
        line_start(o_slot, oz_s, oz_r, 0)
        across(o_slot, ox_s, ox_r, 0)
    share(z, x)

    gain = gain_ref[...]

    def norm_rows(member):
        base = pl.multiple_of(member * rows, rows)

        def body(b, _):
            r0 = pl.multiple_of(b * 64, 64)
            wide = xg[member, pl.ds(r0, 64), :].astype(jnp.float32)
            ms = jnp.mean(wide * wide, axis=-1, keepdims=True)
            out = (wide * lax.rsqrt(ms + EPS) * gain).astype(jnp.bfloat16)
            for g in range(nz):
                normed[g, pl.ds(base + r0, 64), :] = out[:, g * chunk : (g + 1) * chunk]
            return 0

        lax.fori_loop(0, rows // 64, body, 0)

    norm_rows(me)
    for k in range(1, nc):
        other = seq_at(y, (core - k + nc) % nc)
        arrive(xg.at[other], xc_r.at[0, k])
        norm_rows(other)
    for i in range(1, nz - 1):
        w_relay(i)
    for i in range(1, ny):
        yy = (y - i + ny) % ny
        source = seq_at(yy, core)
        arrive(xg.at[source], xy_r.at[i])
        for k in range(1, nc):
            go(remote(xg.at[source], xg.at[source], xc_s.at[i, k], xc_r.at[i, k], dp, seq_at(y, (core + k) % nc)))
        norm_rows(source)
    for i in range(1, ny):
        yy = (y - i + ny) % ny
        for k in range(1, nc):
            other = seq_at(yy, (core - k + nc) % nc)
            arrive(xg.at[other], xc_r.at[i, k])
            norm_rows(other)

    for i in range(1, n):
        arrive(idg.at[(me - i + n) % n], id_r.at[i])
    for m in range(n):
        line = jnp.broadcast_to(idg[m].astype(jnp.float32), (128, rows))
        idcol[pl.ds(m * rows, rows), :] = jnp.transpose(line)
    id_row = jnp.concatenate([idg[m] for m in range(n)], axis=1).astype(jnp.float32)

    row_block = 256
    blocks = seq_len // row_block

    def project(i, first):
        zz = piece(i)
        for k in range(1, nx):
            arrive(w_slot(zz, (x - k + nx) % nx), wx_r.at[zz, k])

        def body(b, _):
            r = pl.ds(pl.multiple_of(b * row_block, row_block), row_block)
            prod = jnp.dot(normed[zz, r, :], wg[zz], preferred_element_type=jnp.float32)
            if first:
                acc[r, :] = prod
            else:
                acc[r, :] = acc[r, :] + prod
            return 0

        lax.fori_loop(0, blocks, body, 0)

    for i in range(nz):
        if i == max(0, nz - 2):
            if nz > 1:
                w_relay(nz - 1)
                if late:
                    line_start(o_slot, oz_s, oz_r, 0)
                    across(o_slot, ox_s, ox_r, 0)
            for e in range(1, nz - 2):
                o_relay(e)
        project(i, i == 0)
    if nz > 2:
        o_relay(nz - 2)

    def group_of(shape, dim):
        return lax.div(lax.broadcasted_iota(jnp.int32, shape, dim), jnp.int32(channel))

    same_head = (group_of((cols, cols), 0) == group_of((cols, cols), 1)).astype(jnp.float32)
    same_head = same_head.astype(jnp.bfloat16)
    scale_row = jnp.zeros((1, cols), jnp.float32)
    for h in range(heads):
        scale_row = jnp.where(group_of((1, cols), 1) == h, scale_ref[me * heads + h], scale_row)
    scale_row = scale_row / math.sqrt(channel)

    def head_scale(values):
        square = values * values
        high = square.astype(jnp.bfloat16)
        low = (square - high.astype(jnp.float32)).astype(jnp.bfloat16)
        total = jnp.dot(high, same_head, preferred_element_type=jnp.float32) + jnp.dot(
            low, same_head, preferred_element_type=jnp.float32
        )
        return lax.rsqrt(total / channel + EPS)

    def split(b, _):
        r = pl.ds(pl.multiple_of(b * row_block, row_block), row_block)
        joined = acc[r, :].astype(jnp.bfloat16)
        q = joined[:, :cols].astype(jnp.float32)
        k = joined[:, cols : 2 * cols].astype(jnp.float32)
        qs[r, :] = (q * head_scale(q) * scale_row).astype(jnp.bfloat16)
        ks[r, :] = (k * head_scale(k)).astype(jnp.bfloat16)
        vs[r, :] = joined[:, 2 * cols :]
        return 0

    lax.fori_loop(0, blocks, split, 0)

    if nz > 1:
        o_relay(nz - 1)
    o_crossed(0)

    q_block = cfg["q_block"]
    lane_head = group_of((q_block, cols), 1)

    def stage_target(t, sign):
        dy = (t // nc + 1) % ny
        dc = (t + 1) % nc
        if sign > 0:
            return seq_at((y + dy) % ny, (core + dc) % nc)
        return seq_at((y - dy + ny) % ny, (core - dc + nc) % nc)

    def a2a(t):
        j = stage_target(t, 1)
        return remote(ao.at[j], ag.at[me], at_s.at[t], at_r.at[t], dp, j)

    def stage(t, _):
        j = stage_target(t, 1)
        for sub in range(rows // q_block):
            r = pl.ds(pl.multiple_of(j * rows + sub * q_block, q_block), q_block)
            bias = jnp.where(idcol[r, :][:, :1] == id_row, 0.0, NEG)
            qb = qs[r, :]
            out = jnp.zeros((q_block, cols), jnp.float32)
            for h in range(heads):
                mine = lane_head == h
                qh = jnp.where(mine, qb, jnp.zeros_like(qb))
                s = lax.dot_general(
                    qh, ks[...], (((1,), (1,)), ((), ())), preferred_element_type=jnp.float32
                )
                s = s + bias
                p = jnp.exp(s - jnp.max(s, axis=-1, keepdims=True))
                total = jnp.sum(p, axis=-1, keepdims=True)
                o = jnp.dot(p.astype(jnp.bfloat16), vs[...], preferred_element_type=jnp.float32)
                out = jnp.where(mine, o / total, out)
            ao[j, pl.ds(sub * q_block, q_block), :] = out.astype(jnp.bfloat16)

        @pl.when(t < n - 1)
        def _():
            a2a(t).start()

        for i in range(1, nz):

            @pl.when(t == min(i - 1, n - 1))
            def _(i=i):
                o_crossed(i)

        return 0

    lax.fori_loop(0, n, stage, 0)

    for k in range(1, nc):
        half = wog.at[(core - k + nc) % nc]
        for d in range(ndp):
            arrive(half.at[pl.ds(d * shard, shard), :], oc_r.at[d, k])
    for t in range(n - 1):
        arrive(ag.at[stage_target(t, -1)], at_r.at[t])
    ag[me] = ao[me]

    attention = jnp.concatenate([ag[m] for m in range(n)], axis=1)
    for g in range(nc):
        lanes = slice(g * (width // nc), (g + 1) * (width // nc))
        prod = jnp.dot(attention, wog[g], preferred_element_type=jnp.float32)
        mixed_ref[:, lanes] = (xg[me, :, lanes].astype(jnp.float32) + prod).astype(jnp.bfloat16)

    logits = lax.dot_general(
        bits_ref[...], mixed_ref[...], (((1,), (1,)), ((), ())), preferred_element_type=jnp.float32
    )
    eye = lax.broadcasted_iota(jnp.int32, (bits, bits), 0) == lax.broadcasted_iota(
        jnp.int32, (bits, bits), 1
    )
    offset = jnp.sum(jnp.where(eye, off_ref[...], 0.0), axis=1, keepdims=True)
    probs = jax.nn.sigmoid(4.0 * (logits + offset))
    part1[me, :, :] = jnp.broadcast_to(jnp.sum(probs, axis=1, keepdims=True), (bits, 128))
    for i in range(1, n):
        go(remote(part1.at[me], part1.at[me], p1_s.at[i], p1_r.at[i], dp, (me + i) % n))
    for i in range(1, n):
        arrive(part1.at[(me - i + n) % n], p1_r.at[i])
    pack = part1[0]
    for m in range(1, n):
        pack = pack + part1[m]
    part2[dp, :, :] = pack
    for i in range(1, ndp):
        go(remote(part2.at[dp], part2.at[dp], p2_s.at[i], p2_r.at[i], (dp + i) % ndp, me))
    for i in range(1, ndp):
        arrive(part2.at[(dp - i + ndp) % ndp], p2_r.at[i])
    total = part2[0]
    for m in range(1, ndp):
        total = total + part2[m]
    marginal = total / (seq_len * ndp)
    line = jnp.sum(jnp.where(eye, marginal[:, :bits], 0.0), axis=0, keepdims=True)
    ent_ref[...] = -(line * jnp.log(line) + (1.0 - line) * jnp.log(1.0 - line))
    codes_ref[...] = probs - marginal[:, :1]

    for c in sends:
        c.wait_send()
    for t in range(n - 1):
        a2a(t).wait_send()
    for d in range(ndp):
        for k in range(1, nc):
            shared(d // nx, d % nx, k).wait_send()
    for cond, c in line_sends:

        @pl.when(cond)
        def _(c=c):
            c.wait_send()


def on_device(
    cfg,
    residual_tiles,
    picture_label_tile,
    prenorm_multiplier,
    triple_projector,
    logit_scaling,
    final_projector,
    binarizer_projector,
    binarizer_offset,
):
    nz, nx, ny, nc = cfg["nz"], cfg["nx"], cfg["ny"], cfg["nc"]
    n, ndp = ny * nc, nz * nx
    _, rows, width = residual_tiles.shape
    heads_all = logit_scaling.shape[0]
    bits = binarizer_projector.shape[1]
    cols = width // n
    shard = triple_projector.shape[0]
    seq_len = rows * n
    cfg = dict(cfg, heads=heads_all // n, channel=width // heads_all, q_block=min(256, rows))
    dma = pltpu.SemaphoreType.DMA
    vmem, hbm = pl.BlockSpec(memory_space=pltpu.VMEM), pl.BlockSpec(memory_space=pl.ANY)
    smem = pl.BlockSpec(memory_space=pltpu.SMEM)
    bf16, f32 = jnp.bfloat16, jnp.float32
    mixed, codes, ent = pl.pallas_call(
        functools.partial(layer_kernel, cfg),
        out_shape=(
            jax.ShapeDtypeStruct((rows, width), bf16),
            jax.ShapeDtypeStruct((bits, rows), f32),
            jax.ShapeDtypeStruct((1, bits), f32),
        ),
        in_specs=[hbm, vmem, vmem, hbm, smem, hbm, vmem, vmem],
        out_specs=(vmem, vmem, vmem),
        scratch_shapes=[
            pltpu.VMEM((nz, nx * shard, 3 * cols), bf16),
            pltpu.VMEM((nc, width, width // nc), bf16),
            pltpu.VMEM((n, rows, width), bf16),
            pltpu.VMEM((n, 1, rows), jnp.int32),
            pltpu.VMEM((seq_len, 128), f32),
            pltpu.VMEM((nz, seq_len, nx * shard), bf16),
            pltpu.VMEM((seq_len, 3 * cols), f32),
            pltpu.VMEM((seq_len, cols), bf16),
            pltpu.VMEM((seq_len, cols), bf16),
            pltpu.VMEM((seq_len, cols), bf16),
            pltpu.VMEM((n, rows, cols), bf16),
            pltpu.VMEM((n, rows, cols), bf16),
            pltpu.VMEM((n, bits, 128), f32),
            pltpu.VMEM((ndp, bits, 128), f32),
            dma((6,)),
            dma((nz + 2,)),
            dma((nz,)),
            dma((nz, nx)),
            dma((nz, nx)),
            dma((nz + 2,)),
            dma((nz,)),
            dma((nz, nx)),
            dma((nz, nx)),
            dma((ndp, nc)),
            dma((ndp, nc)),
            dma((ny,)),
            dma((ny,)),
            dma((ny, nc)),
            dma((ny, nc)),
            dma((n,)),
            dma((n,)),
            dma((n,)),
            dma((n,)),
            dma((n,)),
            dma((n,)),
            dma((ndp,)),
            dma((ndp,)),
        ],
        compiler_params=pltpu.CompilerParams(
            collective_id=0, has_side_effects=True, vmem_limit_bytes=60 * 1024 * 1024
        ),
        name="layer",
    )(
        residual_tiles[0],
        picture_label_tile,
        prenorm_multiplier[None],
        triple_projector,
        logit_scaling,
        final_projector,
        binarizer_projector.T,
        binarizer_offset[None],
    )
    return mixed[None], codes[None], ent[0]


def solution(mesh):
    ndp, n = mesh.shape["dp"], mesh.shape["seq"]
    nx = math.isqrt(ndp // 2)
    if nx < 1 or ndp % nx:
        nx = 1
    nc = 2 if n % 2 == 0 else 1
    cfg = {"nz": ndp // nx, "nx": nx, "ny": n // nc, "nc": nc, "late": False}
    return jax.shard_map(
        functools.partial(on_device, cfg),
        mesh=mesh,
        in_specs=(
            P("dp", "seq", None),
            P("dp", "seq"),
            P(),
            P("dp", None),
            P(),
            P("dp", None),
            P(),
            P(),
        ),
        out_specs=(P("dp", "seq", None), P("dp", None, "seq"), P()),
        check_vma=False,
    )
```

```python
import functools
import math

import jax
import jax.numpy as jnp
from jax import lax
from jax.experimental import pallas as pl
from jax.experimental.pallas import tpu as pltpu
from jax.sharding import PartitionSpec as P

EPS = 1e-06
MESH = pl.DeviceIdType.MESH
NEG = -1e30


def layer_kernel(
    cfg,
    x_ref,
    ids_ref,
    gain_ref,
    w_ref,
    scale_ref,
    wo_ref,
    bits_ref,
    off_ref,
    mixed_ref,
    codes_ref,
    ent_ref,
    wg,
    wog,
    xg,
    idg,
    idcol,
    normed,
    acc,
    qs,
    ks,
    vs,
    ao,
    ag,
    part1,
    part2,
    local_sem,
    wz_s,
    wz_r,
    wx_s,
    wx_r,
    oz_s,
    oz_r,
    ox_s,
    ox_r,
    oc_s,
    oc_r,
    xy_s,
    xy_r,
    xc_s,
    xc_r,
    id_s,
    id_r,
    at_s,
    at_r,
    p1_s,
    p1_r,
    p2_s,
    p2_r,
):
    nz, nx, ny, nc = cfg["nz"], cfg["nx"], cfg["ny"], cfg["nc"]
    n = ny * nc
    ndp = nz * nx
    heads, channel = cfg["heads"], cfg["channel"]
    rows, width = x_ref.shape
    shard = w_ref.shape[0]
    chunk = nx * shard
    cols = width // n
    seq_len = rows * n
    bits = bits_ref.shape[0]
    dp = lax.axis_index("dp")
    me = lax.axis_index("seq")
    z = dp // nx
    x = dp % nx
    y = me // nc
    core = me % nc

    def dp_at(zz, xx):
        return zz * nx + xx

    def seq_at(yy, cc):
        return yy * nc + cc

    def remote(src, dst, ss, rs, d, s):
        return pltpu.make_async_remote_copy(
            src_ref=src, dst_ref=dst, send_sem=ss, recv_sem=rs, device_id=(d, s), device_id_type=MESH
        )

    sends = []

    def go(c):
        c.start()
        sends.append(c)

    def arrive(slot, sem):
        remote(slot, slot, sem, sem, dp, me).wait_recv()

    parts = cfg["parts"]
    piece_rows = shard // parts

    def w_slot_of(h):
        def slot(zz, xx):
            return wg.at[zz, pl.ds(pl.multiple_of(xx * shard + h * piece_rows, piece_rows), piece_rows), :]

        return slot

    w_slots = [w_slot_of(h) for h in range(parts)]
    half_rows = rows // 2

    def x_half(member, h):
        return xg.at[member, pl.ds(h * half_rows, half_rows), :]

    def o_slot(zz, xx):
        return wog.at[core, pl.ds(pl.multiple_of(dp_at(zz, xx) * shard, shard), shard), :]

    lo = jnp.minimum(z, nz - 1 - z)

    def piece(i):
        near = z - (i + 1) // 2 if i % 2 else z + (i + 1) // 2
        far = jnp.where(z > nz - 1 - z, z - (i - lo), z + (i - lo))
        return jnp.where(i <= 2 * lo, near, far) if i else z

    def first_hops(slot, ss, rs):
        left = remote(slot(z, x), slot(z, x), ss.at[nz], rs.at[z], dp_at(jnp.maximum(z - 1, 0), x), me)
        right = remote(
            slot(z, x), slot(z, x), ss.at[nz + 1], rs.at[z], dp_at(jnp.minimum(z + 1, nz - 1), x), me
        )
        return left, right

    def next_hops(slot, ss, rs, i):
        p = piece(i)
        left = remote(slot(p, x), slot(p, x), ss.at[p], rs.at[p], dp_at(jnp.maximum(z - 1, 0), x), me)
        right = remote(
            slot(p, x), slot(p, x), ss.at[p], rs.at[p], dp_at(jnp.minimum(z + 1, nz - 1), x), me
        )
        return left, right

    line_sends = []

    def line_start(slot, ss, rs, i):
        if nz == 1:
            return
        p = piece(i)
        left, right = next_hops(slot, ss, rs, i) if i else first_hops(slot, ss, rs)
        to_left = jnp.logical_and(p >= z, z > 0)
        to_right = jnp.logical_and(p <= z, z < nz - 1)
        line_sends.append((to_left, left))
        line_sends.append((to_right, right))

        @pl.when(to_left)
        def _():
            left.start()

        @pl.when(to_right)
        def _():
            right.start()

    def across(slot, ss, rs, i):
        p = piece(i)
        for k in range(1, nx):
            go(remote(slot(p, x), slot(p, x), ss.at[p, k], rs.at[p, k], dp_at(z, (x + k) % nx), me))

    def shared(p, xx, k):
        idx = dp_at(p, xx)
        slot = o_slot(p, xx)
        return remote(slot, slot, oc_s.at[idx, k], oc_r.at[idx, k], dp, seq_at(y, (core + k) % nc))

    def share(p, xx):
        for k in range(1, nc):
            shared(p, xx, k).start()

    def w_relay(i):
        p = piece(i)
        for h, slot in enumerate(w_slots):
            arrive(slot(p, x), wz_r.at[h, p])
            line_start(slot, wz_s.at[h], wz_r.at[h], i)
            across(slot, wx_s.at[h], wx_r.at[h], i)

    def o_relay(i):
        p = piece(i)
        arrive(o_slot(p, x), oz_r.at[p])
        line_start(o_slot, oz_s, oz_r, i)
        across(o_slot, ox_s, ox_r, i)
        share(p, x)

    def o_crossed(i):
        p = piece(i)
        for k in range(1, nx):
            xx = (x - k + nx) % nx
            arrive(o_slot(p, xx), ox_r.at[p, k])
            share(p, xx)

    own = []
    for part in range(3):
        own.append(
            pltpu.make_async_copy(
                w_ref.at[:, pl.ds(pl.multiple_of(part * width + me * cols, 128), cols)],
                wg.at[
                    z,
                    pl.ds(pl.multiple_of(x * shard, shard), shard),
                    pl.ds(part * cols, cols),
                ],
                local_sem.at[part],
            )
        )
    own.append(pltpu.make_async_copy(x_ref, xg.at[me], local_sem.at[3]))
    own.append(pltpu.make_async_copy(ids_ref, idg.at[me], local_sem.at[4]))
    own.append(
        pltpu.make_async_copy(
            wo_ref.at[:, pl.ds(pl.multiple_of(core * (width // nc), 128), width // nc)],
            o_slot(z, x),
            local_sem.at[5],
        )
    )
    for c in own:
        c.start()

    barrier = pltpu.get_barrier_semaphore()

    def greet_seq(i, _):
        pl.semaphore_signal(
            barrier, inc=1, device_id=(dp, (me + i) % n), device_id_type=MESH
        )
        return 0

    def greet_dp(i, _):
        pl.semaphore_signal(
            barrier, inc=1, device_id=((dp + i) % ndp, me), device_id_type=MESH
        )
        return 0

    lax.fori_loop(1, n, greet_seq, 0)
    lax.fori_loop(1, ndp, greet_dp, 0)
    pl.semaphore_wait(barrier, n - 1 + ndp - 1)

    own[0].wait()
    own[1].wait()
    own[2].wait()
    for h, slot in enumerate(w_slots):
        line_start(slot, wz_s.at[h], wz_r.at[h], 0)
        across(slot, wx_s.at[h], wx_r.at[h], 0)
    own[4].wait()
    for i in range(1, n):
        go(remote(idg.at[me], idg.at[me], id_s.at[i], id_r.at[i], dp, (me + i) % n))
    own[3].wait()
    for h in range(2):
        for i in range(1, ny):
            own_half = x_half(me, h)
            go(remote(own_half, own_half, xy_s.at[h, i], xy_r.at[h, i], dp, seq_at((y + i) % ny, core)))
    for k in range(1, nc):
        go(remote(xg.at[me], xg.at[me], xc_s.at[0, 0, k], xc_r.at[0, 0, k], dp, seq_at(y, (core + k) % nc)))
    own[5].wait()
    line_start(o_slot, oz_s, oz_r, 0)
    across(o_slot, ox_s, ox_r, 0)
    share(z, x)

    gain = gain_ref[...]

    def norm_rows(member, h):
        base = pl.multiple_of(member * rows, rows)

        def body(b, _):
            r0 = pl.multiple_of(h * half_rows + b * 64, 64)
            wide = xg[member, pl.ds(r0, 64), :].astype(jnp.float32)
            ms = jnp.mean(wide * wide, axis=-1, keepdims=True)
            out = (wide * lax.rsqrt(ms + EPS) * gain).astype(jnp.bfloat16)
            for g in range(nz):
                normed[g, pl.ds(base + r0, 64), :] = out[:, g * chunk : (g + 1) * chunk]
            return 0

        lax.fori_loop(0, half_rows // 64, body, 0)

    def x_relay(h):
        for i in range(1, ny):
            source = seq_at((y - i + ny) % ny, core)
            slot = x_half(source, h)
            arrive(slot, xy_r.at[h, i])
            for k in range(1, nc):
                go(remote(slot, slot, xc_s.at[h, i, k], xc_r.at[h, i, k], dp, seq_at(y, (core + k) % nc)))
            norm_rows(source, h)

    def x_shared(h):
        for i in range(1, ny):
            for k in range(1, nc):
                other = seq_at((y - i + ny) % ny, (core - k + nc) % nc)
                arrive(x_half(other, h), xc_r.at[h, i, k])
                norm_rows(other, h)

    for h in range(2):
        norm_rows(me, h)
    for k in range(1, nc):
        other = seq_at(y, (core - k + nc) % nc)
        arrive(xg.at[other], xc_r.at[0, 0, k])
        for h in range(2):
            norm_rows(other, h)
    for i in range(1, nz):
        w_relay(i)
        if i == 1:
            x_relay(0)
    if nz == 1:
        x_relay(0)
    x_relay(1)
    for h in range(2):
        x_shared(h)

    for i in range(1, n):
        arrive(idg.at[(me - i + n) % n], id_r.at[i])
    for m in range(n):
        line = jnp.broadcast_to(idg[m].astype(jnp.float32), (128, rows))
        idcol[pl.ds(m * rows, rows), :] = jnp.transpose(line)
    id_row = jnp.concatenate([idg[m] for m in range(n)], axis=1).astype(jnp.float32)

    row_block = 256
    blocks = seq_len // row_block

    def project(i, first):
        zz = piece(i)
        for k in range(1, nx):
            for h, slot in enumerate(w_slots):
                arrive(slot(zz, (x - k + nx) % nx), wx_r.at[h, zz, k])

        def body(b, _):
            r = pl.ds(pl.multiple_of(b * row_block, row_block), row_block)
            prod = jnp.dot(normed[zz, r, :], wg[zz], preferred_element_type=jnp.float32)
            if first:
                acc[r, :] = prod
            else:
                acc[r, :] = acc[r, :] + prod
            return 0

        lax.fori_loop(0, blocks, body, 0)

    for i in range(nz):
        if i == max(0, nz - 2):
            for e in range(1, nz - 2):
                o_relay(e)
        project(i, i == 0)
    if nz > 2:
        o_relay(nz - 2)

    def group_of(shape, dim):
        return lax.div(lax.broadcasted_iota(jnp.int32, shape, dim), jnp.int32(channel))

    same_head = (group_of((cols, cols), 0) == group_of((cols, cols), 1)).astype(jnp.float32)
    same_head = same_head.astype(jnp.bfloat16)
    scale_row = jnp.zeros((1, cols), jnp.float32)
    for h in range(heads):
        scale_row = jnp.where(group_of((1, cols), 1) == h, scale_ref[me * heads + h], scale_row)
    scale_row = scale_row / math.sqrt(channel)

    def head_scale(values):
        square = values * values
        high = square.astype(jnp.bfloat16)
        low = (square - high.astype(jnp.float32)).astype(jnp.bfloat16)
        total = jnp.dot(high, same_head, preferred_element_type=jnp.float32) + jnp.dot(
            low, same_head, preferred_element_type=jnp.float32
        )
        return lax.rsqrt(total / channel + EPS)

    def split(b, _):
        r = pl.ds(pl.multiple_of(b * row_block, row_block), row_block)
        joined = acc[r, :].astype(jnp.bfloat16)
        q = joined[:, :cols].astype(jnp.float32)
        k = joined[:, cols : 2 * cols].astype(jnp.float32)
        qs[r, :] = (q * head_scale(q) * scale_row).astype(jnp.bfloat16)
        ks[r, :] = (k * head_scale(k)).astype(jnp.bfloat16)
        vs[r, :] = joined[:, 2 * cols :]
        return 0

    lax.fori_loop(0, blocks, split, 0)

    if nz > 1:
        o_relay(nz - 1)
    o_crossed(0)

    q_block = cfg["q_block"]
    lane_head = group_of((q_block, cols), 1)

    def stage_target(t, sign):
        dy = (t // nc + 1) % ny
        dc = (t + 1) % nc
        if sign > 0:
            return seq_at((y + dy) % ny, (core + dc) % nc)
        return seq_at((y - dy + ny) % ny, (core - dc + nc) % nc)

    def a2a(t):
        j = stage_target(t, 1)
        return remote(ao.at[j], ag.at[me], at_s.at[t], at_r.at[t], dp, j)

    def stage(t, _):
        j = stage_target(t, 1)
        for sub in range(rows // q_block):
            r = pl.ds(pl.multiple_of(j * rows + sub * q_block, q_block), q_block)
            bias = jnp.where(idcol[r, :][:, :1] == id_row, 0.0, NEG)
            qb = qs[r, :]
            out = jnp.zeros((q_block, cols), jnp.float32)
            for h in range(heads):
                mine = lane_head == h
                qh = jnp.where(mine, qb, jnp.zeros_like(qb))
                s = lax.dot_general(
                    qh, ks[...], (((1,), (1,)), ((), ())), preferred_element_type=jnp.float32
                )
                s = s + bias
                p = jnp.exp(s - jnp.max(s, axis=-1, keepdims=True))
                total = jnp.sum(p, axis=-1, keepdims=True)
                o = jnp.dot(p.astype(jnp.bfloat16), vs[...], preferred_element_type=jnp.float32)
                out = jnp.where(mine, o / total, out)
            ao[j, pl.ds(sub * q_block, q_block), :] = out.astype(jnp.bfloat16)

        @pl.when(t < n - 1)
        def _():
            a2a(t).start()

        for i in range(1, nz):

            @pl.when(t == min(i - 1, n - 1))
            def _(i=i):
                o_crossed(i)

        return 0

    lax.fori_loop(0, n, stage, 0)

    for k in range(1, nc):
        half = wog.at[(core - k + nc) % nc]
        for d in range(ndp):
            arrive(half.at[pl.ds(d * shard, shard), :], oc_r.at[d, k])
    for t in range(n - 1):
        arrive(ag.at[stage_target(t, -1)], at_r.at[t])
    ag[me] = ao[me]

    attention = jnp.concatenate([ag[m] for m in range(n)], axis=1)
    for g in range(nc):
        lanes = slice(g * (width // nc), (g + 1) * (width // nc))
        prod = jnp.dot(attention, wog[g], preferred_element_type=jnp.float32)
        mixed_ref[:, lanes] = (xg[me, :, lanes].astype(jnp.float32) + prod).astype(jnp.bfloat16)

    logits = lax.dot_general(
        bits_ref[...], mixed_ref[...], (((1,), (1,)), ((), ())), preferred_element_type=jnp.float32
    )
    eye = lax.broadcasted_iota(jnp.int32, (bits, bits), 0) == lax.broadcasted_iota(
        jnp.int32, (bits, bits), 1
    )
    offset = jnp.sum(jnp.where(eye, off_ref[...], 0.0), axis=1, keepdims=True)
    probs = jax.nn.sigmoid(4.0 * (logits + offset))
    part1[me, :, :] = jnp.broadcast_to(jnp.sum(probs, axis=1, keepdims=True), (bits, 128))
    for i in range(1, n):
        go(remote(part1.at[me], part1.at[me], p1_s.at[i], p1_r.at[i], dp, (me + i) % n))
    for i in range(1, n):
        arrive(part1.at[(me - i + n) % n], p1_r.at[i])
    pack = part1[0]
    for m in range(1, n):
        pack = pack + part1[m]
    part2[dp, :, :] = pack
    for i in range(1, ndp):
        go(remote(part2.at[dp], part2.at[dp], p2_s.at[i], p2_r.at[i], (dp + i) % ndp, me))
    for i in range(1, ndp):
        arrive(part2.at[(dp - i + ndp) % ndp], p2_r.at[i])
    total = part2[0]
    for m in range(1, ndp):
        total = total + part2[m]
    marginal = total / (seq_len * ndp)
    line = jnp.sum(jnp.where(eye, marginal[:, :bits], 0.0), axis=0, keepdims=True)
    ent_ref[...] = -(line * jnp.log(line) + (1.0 - line) * jnp.log(1.0 - line))
    codes_ref[...] = probs - marginal[:, :1]

    for c in sends:
        c.wait_send()
    for t in range(n - 1):
        a2a(t).wait_send()
    for d in range(ndp):
        for k in range(1, nc):
            shared(d // nx, d % nx, k).wait_send()
    for cond, c in line_sends:

        @pl.when(cond)
        def _(c=c):
            c.wait_send()


def on_device(
    cfg,
    residual_tiles,
    picture_label_tile,
    prenorm_multiplier,
    triple_projector,
    logit_scaling,
    final_projector,
    binarizer_projector,
    binarizer_offset,
):
    nz, nx, ny, nc = cfg["nz"], cfg["nx"], cfg["ny"], cfg["nc"]
    n, ndp = ny * nc, nz * nx
    _, rows, width = residual_tiles.shape
    heads_all = logit_scaling.shape[0]
    bits = binarizer_projector.shape[1]
    cols = width // n
    shard = triple_projector.shape[0]
    seq_len = rows * n
    parts = 2 if shard % 32 == 0 else 1
    cfg = dict(cfg, heads=heads_all // n, channel=width // heads_all, q_block=min(256, rows), parts=parts)
    dma = pltpu.SemaphoreType.DMA
    vmem, hbm = pl.BlockSpec(memory_space=pltpu.VMEM), pl.BlockSpec(memory_space=pl.ANY)
    smem = pl.BlockSpec(memory_space=pltpu.SMEM)
    bf16, f32 = jnp.bfloat16, jnp.float32
    mixed, codes, ent = pl.pallas_call(
        functools.partial(layer_kernel, cfg),
        out_shape=(
            jax.ShapeDtypeStruct((rows, width), bf16),
            jax.ShapeDtypeStruct((bits, rows), f32),
            jax.ShapeDtypeStruct((1, bits), f32),
        ),
        in_specs=[hbm, vmem, vmem, hbm, smem, hbm, vmem, vmem],
        out_specs=(vmem, vmem, vmem),
        scratch_shapes=[
            pltpu.VMEM((nz, nx * shard, 3 * cols), bf16),
            pltpu.VMEM((nc, width, width // nc), bf16),
            pltpu.VMEM((n, rows, width), bf16),
            pltpu.VMEM((n, 1, rows), jnp.int32),
            pltpu.VMEM((seq_len, 128), f32),
            pltpu.VMEM((nz, seq_len, nx * shard), bf16),
            pltpu.VMEM((seq_len, 3 * cols), f32),
            pltpu.VMEM((seq_len, cols), bf16),
            pltpu.VMEM((seq_len, cols), bf16),
            pltpu.VMEM((seq_len, cols), bf16),
            pltpu.VMEM((n, rows, cols), bf16),
            pltpu.VMEM((n, rows, cols), bf16),
            pltpu.VMEM((n, bits, 128), f32),
            pltpu.VMEM((ndp, bits, 128), f32),
            dma((6,)),
            dma((parts, nz + 2)),
            dma((parts, nz)),
            dma((parts, nz, nx)),
            dma((parts, nz, nx)),
            dma((nz + 2,)),
            dma((nz,)),
            dma((nz, nx)),
            dma((nz, nx)),
            dma((ndp, nc)),
            dma((ndp, nc)),
            dma((2, ny)),
            dma((2, ny)),
            dma((2, ny, nc)),
            dma((2, ny, nc)),
            dma((n,)),
            dma((n,)),
            dma((n,)),
            dma((n,)),
            dma((n,)),
            dma((n,)),
            dma((ndp,)),
            dma((ndp,)),
        ],
        compiler_params=pltpu.CompilerParams(
            collective_id=0, has_side_effects=True, vmem_limit_bytes=60 * 1024 * 1024
        ),
        name="layer",
    )(
        residual_tiles[0],
        picture_label_tile,
        prenorm_multiplier[None],
        triple_projector,
        logit_scaling,
        final_projector,
        binarizer_projector.T,
        binarizer_offset[None],
    )
    return mixed[None], codes[None], ent[0]


def solution(mesh):
    ndp, n = mesh.shape["dp"], mesh.shape["seq"]
    nx = math.isqrt(ndp // 2)
    if nx < 1 or ndp % nx:
        nx = 1
    nc = 2 if n % 2 == 0 else 1
    cfg = {"nz": ndp // nx, "nx": nx, "ny": n // nc, "nc": nc}
    return jax.shard_map(
        functools.partial(on_device, cfg),
        mesh=mesh,
        in_specs=(
            P("dp", "seq", None),
            P("dp", "seq"),
            P(),
            P("dp", None),
            P(),
            P("dp", None),
            P(),
            P(),
        ),
        out_specs=(P("dp", "seq", None), P("dp", None, "seq"), P()),
        check_vma=False,
    )
```

```python
import functools
import math

import jax
import jax.numpy as jnp
from jax import lax
from jax.experimental import pallas as pl
from jax.experimental.pallas import tpu as pltpu
from jax.sharding import PartitionSpec as P

EPS = 1e-06
MESH = pl.DeviceIdType.MESH
NEG = -1e30


def layer_kernel(
    cfg,
    x_ref,
    ids_ref,
    gain_ref,
    w_ref,
    scale_ref,
    wo_ref,
    bits_ref,
    off_ref,
    mixed_ref,
    codes_ref,
    ent_ref,
    wg,
    wog,
    xg,
    idg,
    idcol,
    normed,
    acc,
    qs,
    ks,
    vs,
    ao,
    ag,
    part1,
    part2,
    local_sem,
    wz_s,
    wz_r,
    wx_s,
    wx_r,
    oz_s,
    oz_r,
    ox_s,
    ox_r,
    oc_s,
    oc_r,
    xy_s,
    xy_r,
    xc_s,
    xc_r,
    id_s,
    id_r,
    at_s,
    at_r,
    p1_s,
    p1_r,
    p2_s,
    p2_r,
):
    nz, nx, ny, nc = cfg["nz"], cfg["nx"], cfg["ny"], cfg["nc"]
    n = ny * nc
    ndp = nz * nx
    heads, channel = cfg["heads"], cfg["channel"]
    rows, width = x_ref.shape
    shard = w_ref.shape[0]
    chunk = nx * shard
    cols = width // n
    seq_len = rows * n
    bits = bits_ref.shape[0]
    dp = lax.axis_index("dp")
    me = lax.axis_index("seq")
    z = dp // nx
    x = dp % nx
    y = me // nc
    core = me % nc

    def dp_at(zz, xx):
        return zz * nx + xx

    def seq_at(yy, cc):
        return yy * nc + cc

    def remote(src, dst, ss, rs, d, s):
        return pltpu.make_async_remote_copy(
            src_ref=src, dst_ref=dst, send_sem=ss, recv_sem=rs, device_id=(d, s), device_id_type=MESH
        )

    sends = []

    def go(c):
        c.start()
        sends.append(c)

    def arrive(slot, sem):
        remote(slot, slot, sem, sem, dp, me).wait_recv()

    parts = cfg["parts"]
    piece_rows = shard // parts

    def w_slot_of(h):
        def slot(zz, xx):
            return wg.at[zz, pl.ds(pl.multiple_of(xx * shard + h * piece_rows, piece_rows), piece_rows), :]

        return slot

    w_slots = [w_slot_of(h) for h in range(parts)]
    half_rows = rows // 2

    def x_half(member, h):
        return xg.at[member, pl.ds(h * half_rows, half_rows), :]

    def o_slot(zz, xx):
        return wog.at[core, pl.ds(pl.multiple_of(dp_at(zz, xx) * shard, shard), shard), :]

    lo = jnp.minimum(z, nz - 1 - z)

    def piece(i):
        near = z - (i + 1) // 2 if i % 2 else z + (i + 1) // 2
        far = jnp.where(z > nz - 1 - z, z - (i - lo), z + (i - lo))
        return jnp.where(i <= 2 * lo, near, far) if i else z

    def first_hops(slot, ss, rs):
        left = remote(slot(z, x), slot(z, x), ss.at[nz], rs.at[z], dp_at(jnp.maximum(z - 1, 0), x), me)
        right = remote(
            slot(z, x), slot(z, x), ss.at[nz + 1], rs.at[z], dp_at(jnp.minimum(z + 1, nz - 1), x), me
        )
        return left, right

    def next_hops(slot, ss, rs, i):
        p = piece(i)
        left = remote(slot(p, x), slot(p, x), ss.at[p], rs.at[p], dp_at(jnp.maximum(z - 1, 0), x), me)
        right = remote(
            slot(p, x), slot(p, x), ss.at[p], rs.at[p], dp_at(jnp.minimum(z + 1, nz - 1), x), me
        )
        return left, right

    line_sends = []

    def line_start(slot, ss, rs, i):
        if nz == 1:
            return
        p = piece(i)
        left, right = next_hops(slot, ss, rs, i) if i else first_hops(slot, ss, rs)
        to_left = jnp.logical_and(p >= z, z > 0)
        to_right = jnp.logical_and(p <= z, z < nz - 1)
        line_sends.append((to_left, left))
        line_sends.append((to_right, right))

        @pl.when(to_left)
        def _():
            left.start()

        @pl.when(to_right)
        def _():
            right.start()

    def across(slot, ss, rs, i):
        p = piece(i)
        for k in range(1, nx):
            go(remote(slot(p, x), slot(p, x), ss.at[p, k], rs.at[p, k], dp_at(z, (x + k) % nx), me))

    def shared(p, xx, k):
        idx = dp_at(p, xx)
        slot = o_slot(p, xx)
        return remote(slot, slot, oc_s.at[idx, k], oc_r.at[idx, k], dp, seq_at(y, (core + k) % nc))

    def share(p, xx):
        for k in range(1, nc):
            shared(p, xx, k).start()

    def w_relay(i):
        p = piece(i)
        for h, slot in enumerate(w_slots):
            arrive(slot(p, x), wz_r.at[h, p])
            line_start(slot, wz_s.at[h], wz_r.at[h], i)
            across(slot, wx_s.at[h], wx_r.at[h], i)

    def o_relay(i):
        p = piece(i)
        arrive(o_slot(p, x), oz_r.at[p])
        line_start(o_slot, oz_s, oz_r, i)
        across(o_slot, ox_s, ox_r, i)
        share(p, x)

    def o_crossed(i):
        p = piece(i)
        for k in range(1, nx):
            xx = (x - k + nx) % nx
            arrive(o_slot(p, xx), ox_r.at[p, k])
            share(p, xx)

    own = []
    for part in range(3):
        own.append(
            pltpu.make_async_copy(
                w_ref.at[:, pl.ds(pl.multiple_of(part * width + me * cols, 128), cols)],
                wg.at[
                    z,
                    pl.ds(pl.multiple_of(x * shard, shard), shard),
                    pl.ds(part * cols, cols),
                ],
                local_sem.at[part],
            )
        )
    own.append(pltpu.make_async_copy(x_ref, xg.at[me], local_sem.at[3]))
    own.append(pltpu.make_async_copy(ids_ref, idg.at[me], local_sem.at[4]))
    own.append(
        pltpu.make_async_copy(
            wo_ref.at[:, pl.ds(pl.multiple_of(core * (width // nc), 128), width // nc)],
            o_slot(z, x),
            local_sem.at[5],
        )
    )
    for c in own:
        c.start()

    barrier = pltpu.get_barrier_semaphore()

    def greet_seq(i, _):
        pl.semaphore_signal(
            barrier, inc=1, device_id=(dp, (me + i) % n), device_id_type=MESH
        )
        return 0

    def greet_dp(i, _):
        pl.semaphore_signal(
            barrier, inc=1, device_id=((dp + i) % ndp, me), device_id_type=MESH
        )
        return 0

    lax.fori_loop(1, n, greet_seq, 0)
    lax.fori_loop(1, ndp, greet_dp, 0)
    pl.semaphore_wait(barrier, n - 1 + ndp - 1)

    own[0].wait()
    own[1].wait()
    own[2].wait()
    for h, slot in enumerate(w_slots):
        line_start(slot, wz_s.at[h], wz_r.at[h], 0)
        across(slot, wx_s.at[h], wx_r.at[h], 0)
    own[4].wait()
    for i in range(1, n):
        go(remote(idg.at[me], idg.at[me], id_s.at[i], id_r.at[i], dp, (me + i) % n))
    own[3].wait()
    for h in range(2):
        for i in range(1, ny):
            own_half = x_half(me, h)
            go(remote(own_half, own_half, xy_s.at[h, i], xy_r.at[h, i], dp, seq_at((y + i) % ny, core)))
    for k in range(1, nc):
        go(remote(xg.at[me], xg.at[me], xc_s.at[0, 0, k], xc_r.at[0, 0, k], dp, seq_at(y, (core + k) % nc)))
    own[5].wait()
    line_start(o_slot, oz_s, oz_r, 0)
    across(o_slot, ox_s, ox_r, 0)
    share(z, x)

    gain = gain_ref[...]

    def norm_rows(member, h):
        base = pl.multiple_of(member * rows, rows)

        def body(b, _):
            r0 = pl.multiple_of(h * half_rows + b * 64, 64)
            wide = xg[member, pl.ds(r0, 64), :].astype(jnp.float32)
            ms = jnp.mean(wide * wide, axis=-1, keepdims=True)
            out = (wide * lax.rsqrt(ms + EPS) * gain).astype(jnp.bfloat16)
            for g in range(nz):
                normed[g, pl.ds(base + r0, 64), :] = out[:, g * chunk : (g + 1) * chunk]
            return 0

        lax.fori_loop(0, half_rows // 64, body, 0)

    def x_relay(h):
        for i in range(1, ny):
            source = seq_at((y - i + ny) % ny, core)
            slot = x_half(source, h)
            arrive(slot, xy_r.at[h, i])
            for k in range(1, nc):
                go(remote(slot, slot, xc_s.at[h, i, k], xc_r.at[h, i, k], dp, seq_at(y, (core + k) % nc)))
            norm_rows(source, h)

    def x_shared(h):
        for i in range(1, ny):
            for k in range(1, nc):
                other = seq_at((y - i + ny) % ny, (core - k + nc) % nc)
                arrive(x_half(other, h), xc_r.at[h, i, k])
                norm_rows(other, h)

    for h in range(2):
        norm_rows(me, h)
    for k in range(1, nc):
        other = seq_at(y, (core - k + nc) % nc)
        arrive(xg.at[other], xc_r.at[0, 0, k])
        for h in range(2):
            norm_rows(other, h)
    for i in range(1, nz):
        w_relay(i)
        if i == 1:
            x_relay(0)
    if nz == 1:
        x_relay(0)
    x_relay(1)
    for h in range(2):
        x_shared(h)

    for i in range(1, n):
        arrive(idg.at[(me - i + n) % n], id_r.at[i])
    for m in range(n):
        line = jnp.broadcast_to(idg[m].astype(jnp.float32), (128, rows))
        idcol[pl.ds(m * rows, rows), :] = jnp.transpose(line)
    id_row = jnp.concatenate([idg[m] for m in range(n)], axis=1).astype(jnp.float32)

    row_block = 256
    blocks = seq_len // row_block

    def project(i, first):
        zz = piece(i)
        for k in range(1, nx):
            for h, slot in enumerate(w_slots):
                arrive(slot(zz, (x - k + nx) % nx), wx_r.at[h, zz, k])

        def body(b, _):
            r = pl.ds(pl.multiple_of(b * row_block, row_block), row_block)
            prod = jnp.dot(normed[zz, r, :], wg[zz], preferred_element_type=jnp.float32)
            if first:
                acc[r, :] = prod
            else:
                acc[r, :] = acc[r, :] + prod
            return 0

        lax.fori_loop(0, blocks, body, 0)

    for i in range(nz):
        if i == max(0, nz - 2):
            for e in range(1, nz - 2):
                o_relay(e)
        project(i, i == 0)
    if nz > 2:
        o_relay(nz - 2)

    def group_of(shape, dim):
        return lax.div(lax.broadcasted_iota(jnp.int32, shape, dim), jnp.int32(channel))

    same_head = (group_of((cols, cols), 0) == group_of((cols, cols), 1)).astype(jnp.float32)
    same_head = same_head.astype(jnp.bfloat16)
    scale_row = jnp.zeros((1, cols), jnp.float32)
    for h in range(heads):
        scale_row = jnp.where(group_of((1, cols), 1) == h, scale_ref[me * heads + h], scale_row)
    scale_row = scale_row / math.sqrt(channel)

    def head_scale(values):
        square = values * values
        high = square.astype(jnp.bfloat16)
        low = (square - high.astype(jnp.float32)).astype(jnp.bfloat16)
        total = jnp.dot(high, same_head, preferred_element_type=jnp.float32) + jnp.dot(
            low, same_head, preferred_element_type=jnp.float32
        )
        return lax.rsqrt(total / channel + EPS)

    def split(b, _):
        r = pl.ds(pl.multiple_of(b * row_block, row_block), row_block)
        joined = acc[r, :].astype(jnp.bfloat16)
        q = joined[:, :cols].astype(jnp.float32)
        k = joined[:, cols : 2 * cols].astype(jnp.float32)
        qs[r, :] = (q * head_scale(q) * scale_row).astype(jnp.bfloat16)
        ks[r, :] = (k * head_scale(k)).astype(jnp.bfloat16)
        vs[r, :] = joined[:, 2 * cols :]
        return 0

    lax.fori_loop(0, blocks, split, 0)

    if nz > 1:
        o_relay(nz - 1)
    o_crossed(0)

    q_block = cfg["q_block"]
    lane_head = group_of((q_block, cols), 1)

    def stage_target(t, sign):
        dy = (t // nc + 1) % ny
        dc = (t + 1) % nc
        if sign > 0:
            return seq_at((y + dy) % ny, (core + dc) % nc)
        return seq_at((y - dy + ny) % ny, (core - dc + nc) % nc)

    def a2a(t):
        j = stage_target(t, 1)
        return remote(ao.at[j], ag.at[me], at_s.at[t], at_r.at[t], dp, j)

    def stage(t, _):
        j = stage_target(t, 1)
        for sub in range(rows // q_block):
            r = pl.ds(pl.multiple_of(j * rows + sub * q_block, q_block), q_block)
            bias = jnp.where(idcol[r, :][:, :1] == id_row, 0.0, NEG)
            qb = qs[r, :]
            out = jnp.zeros((q_block, cols), jnp.float32)
            for h in range(heads):
                mine = lane_head == h
                qh = jnp.where(mine, qb, jnp.zeros_like(qb))
                s = lax.dot_general(
                    qh, ks[...], (((1,), (1,)), ((), ())), preferred_element_type=jnp.float32
                )
                s = s + bias
                p = jnp.exp(s - jnp.max(s, axis=-1, keepdims=True))
                total = jnp.sum(p, axis=-1, keepdims=True)
                o = jnp.dot(p.astype(jnp.bfloat16), vs[...], preferred_element_type=jnp.float32)
                out = jnp.where(mine, o / total, out)
            ao[j, pl.ds(sub * q_block, q_block), :] = out.astype(jnp.bfloat16)

        @pl.when(t < n - 1)
        def _():
            a2a(t).start()

        for i in range(1, nz):

            @pl.when(t == min(i - 1, n - 1))
            def _(i=i):
                o_crossed(i)

        return 0

    lax.fori_loop(0, n, stage, 0)

    for k in range(1, nc):
        half = wog.at[(core - k + nc) % nc]
        for d in range(ndp):
            arrive(half.at[pl.ds(d * shard, shard), :], oc_r.at[d, k])
    for t in range(n - 1):
        arrive(ag.at[stage_target(t, -1)], at_r.at[t])
    ag[me] = ao[me]

    attention = jnp.concatenate([ag[m] for m in range(n)], axis=1)
    for g in range(nc):
        lanes = slice(g * (width // nc), (g + 1) * (width // nc))
        prod = jnp.dot(attention, wog[g], preferred_element_type=jnp.float32)
        mixed_ref[:, lanes] = (xg[me, :, lanes].astype(jnp.float32) + prod).astype(jnp.bfloat16)

    logits = lax.dot_general(
        bits_ref[...], mixed_ref[...], (((1,), (1,)), ((), ())), preferred_element_type=jnp.float32
    )
    eye = lax.broadcasted_iota(jnp.int32, (bits, bits), 0) == lax.broadcasted_iota(
        jnp.int32, (bits, bits), 1
    )
    offset = jnp.sum(jnp.where(eye, off_ref[...], 0.0), axis=1, keepdims=True)
    probs = jax.nn.sigmoid(4.0 * (logits + offset))
    lanes_eye = lax.broadcasted_iota(jnp.int32, (bits, 128), 0) == lax.broadcasted_iota(
        jnp.int32, (bits, 128), 1
    )
    own_sums = jnp.sum(probs, axis=1, keepdims=True)
    part1[me, :, :] = jnp.sum(jnp.where(lanes_eye, own_sums, 0.0), axis=0, keepdims=True)
    for i in range(1, n):
        go(remote(part1.at[me], part1.at[me], p1_s.at[i], p1_r.at[i], dp, (me + i) % n))
    for i in range(1, n):
        arrive(part1.at[(me - i + n) % n], p1_r.at[i])
    pack = part1[0]
    for m in range(1, n):
        pack = pack + part1[m]
    part2[dp, :, :] = pack
    for i in range(1, ndp):
        go(remote(part2.at[dp], part2.at[dp], p2_s.at[i], p2_r.at[i], (dp + i) % ndp, me))
    for i in range(1, ndp):
        arrive(part2.at[(dp - i + ndp) % ndp], p2_r.at[i])
    total = part2[0]
    for m in range(1, ndp):
        total = total + part2[m]
    marginal = total / (seq_len * ndp)
    line = marginal[:, :bits]
    ent_ref[...] = -(line * jnp.log(line) + (1.0 - line) * jnp.log(1.0 - line))
    codes = probs - jnp.sum(jnp.where(lanes_eye, marginal, 0.0), axis=1, keepdims=True)
    for b in range(bits):
        codes_ref[b] = codes[b : b + 1, :]

    for c in sends:
        c.wait_send()
    for t in range(n - 1):
        a2a(t).wait_send()
    for d in range(ndp):
        for k in range(1, nc):
            shared(d // nx, d % nx, k).wait_send()
    for cond, c in line_sends:

        @pl.when(cond)
        def _(c=c):
            c.wait_send()


def on_device(
    cfg,
    residual_tiles,
    picture_label_tile,
    prenorm_multiplier,
    triple_projector,
    logit_scaling,
    final_projector,
    binarizer_projector,
    binarizer_offset,
):
    nz, nx, ny, nc = cfg["nz"], cfg["nx"], cfg["ny"], cfg["nc"]
    n, ndp = ny * nc, nz * nx
    _, rows, width = residual_tiles.shape
    heads_all = logit_scaling.shape[0]
    bits = binarizer_projector.shape[1]
    cols = width // n
    shard = triple_projector.shape[0]
    seq_len = rows * n
    parts = 2 if shard % 32 == 0 else 1
    cfg = dict(cfg, heads=heads_all // n, channel=width // heads_all, q_block=min(256, rows), parts=parts)
    dma = pltpu.SemaphoreType.DMA
    vmem, hbm = pl.BlockSpec(memory_space=pltpu.VMEM), pl.BlockSpec(memory_space=pl.ANY)
    smem = pl.BlockSpec(memory_space=pltpu.SMEM)
    bf16, f32 = jnp.bfloat16, jnp.float32
    mixed, codes, ent = pl.pallas_call(
        functools.partial(layer_kernel, cfg),
        out_shape=(
            jax.ShapeDtypeStruct((rows, width), bf16),
            jax.ShapeDtypeStruct((bits, 1, rows), f32),
            jax.ShapeDtypeStruct((1, bits), f32),
        ),
        in_specs=[hbm, vmem, vmem, hbm, smem, hbm, vmem, vmem],
        out_specs=(vmem, vmem, vmem),
        scratch_shapes=[
            pltpu.VMEM((nz, nx * shard, 3 * cols), bf16),
            pltpu.VMEM((nc, width, width // nc), bf16),
            pltpu.VMEM((n, rows, width), bf16),
            pltpu.VMEM((n, 1, rows), jnp.int32),
            pltpu.VMEM((seq_len, 128), f32),
            pltpu.VMEM((nz, seq_len, nx * shard), bf16),
            pltpu.VMEM((seq_len, 3 * cols), f32),
            pltpu.VMEM((seq_len, cols), bf16),
            pltpu.VMEM((seq_len, cols), bf16),
            pltpu.VMEM((seq_len, cols), bf16),
            pltpu.VMEM((n, rows, cols), bf16),
            pltpu.VMEM((n, rows, cols), bf16),
            pltpu.VMEM((n, 1, 128), f32),
            pltpu.VMEM((ndp, 1, 128), f32),
            dma((6,)),
            dma((parts, nz + 2)),
            dma((parts, nz)),
            dma((parts, nz, nx)),
            dma((parts, nz, nx)),
            dma((nz + 2,)),
            dma((nz,)),
            dma((nz, nx)),
            dma((nz, nx)),
            dma((ndp, nc)),
            dma((ndp, nc)),
            dma((2, ny)),
            dma((2, ny)),
            dma((2, ny, nc)),
            dma((2, ny, nc)),
            dma((n,)),
            dma((n,)),
            dma((n,)),
            dma((n,)),
            dma((n,)),
            dma((n,)),
            dma((ndp,)),
            dma((ndp,)),
        ],
        compiler_params=pltpu.CompilerParams(
            collective_id=0, has_side_effects=True, vmem_limit_bytes=60 * 1024 * 1024
        ),
        name="layer",
    )(
        residual_tiles[0],
        picture_label_tile,
        prenorm_multiplier[None],
        triple_projector,
        logit_scaling,
        final_projector,
        binarizer_projector.T,
        binarizer_offset[None],
    )
    return mixed[None], jnp.swapaxes(codes, 0, 1), ent[0]


def solution(mesh):
    ndp, n = mesh.shape["dp"], mesh.shape["seq"]
    nx = math.isqrt(ndp // 2)
    if nx < 1 or ndp % nx:
        nx = 1
    nc = 2 if n % 2 == 0 else 1
    cfg = {"nz": ndp // nx, "nx": nx, "ny": n // nc, "nc": nc}
    return jax.shard_map(
        functools.partial(on_device, cfg),
        mesh=mesh,
        in_specs=(
            P("dp", "seq", None),
            P("dp", "seq"),
            P(),
            P("dp", None),
            P(),
            P("dp", None),
            P(),
            P(),
        ),
        out_specs=(P("dp", "seq", None), P("dp", None, "seq"), P()),
        check_vma=False,
    )
```

```python
import functools
import math

import jax
import jax.numpy as jnp
from jax import lax
from jax.experimental import pallas as pl
from jax.experimental.pallas import tpu as pltpu
from jax.sharding import PartitionSpec as P

EPS = 1e-06
MESH = pl.DeviceIdType.MESH
NEG = -1e30


def layer_kernel(
    cfg,
    x_ref,
    ids_ref,
    gain_ref,
    w_ref,
    scale_ref,
    wo_ref,
    bits_ref,
    off_ref,
    mixed_ref,
    codes_ref,
    ent_ref,
    wg,
    wog,
    xg,
    idg,
    idcol,
    normed,
    acc,
    qs,
    ks,
    vs,
    ao,
    ag,
    part1,
    part2,
    local_sem,
    wz_s,
    wz_r,
    wx_s,
    wx_r,
    oz_s,
    oz_r,
    ox_s,
    ox_r,
    oc_s,
    oc_r,
    xy_s,
    xy_r,
    xc_s,
    xc_r,
    id_s,
    id_r,
    at_s,
    at_r,
    p1_s,
    p1_r,
    p2_s,
    p2_r,
):
    nz, nx, ny, nc = cfg["nz"], cfg["nx"], cfg["ny"], cfg["nc"]
    n = ny * nc
    ndp = nz * nx
    heads, channel = cfg["heads"], cfg["channel"]
    rows, width = x_ref.shape
    shard = w_ref.shape[0]
    chunk = nx * shard
    cols = width // n
    seq_len = rows * n
    bits = bits_ref.shape[0]
    dp = lax.axis_index("dp")
    me = lax.axis_index("seq")
    z = dp // nx
    x = dp % nx
    y = me // nc
    core = me % nc

    def dp_at(zz, xx):
        return zz * nx + xx

    def seq_at(yy, cc):
        return yy * nc + cc

    def remote(src, dst, ss, rs, d, s):
        return pltpu.make_async_remote_copy(
            src_ref=src, dst_ref=dst, send_sem=ss, recv_sem=rs, device_id=(d, s), device_id_type=MESH
        )

    sends = []

    def go(c):
        c.start()
        sends.append(c)

    def arrive(slot, sem):
        remote(slot, slot, sem, sem, dp, me).wait_recv()

    parts = cfg["parts"]
    piece_rows = shard // parts

    def w_slot_of(h):
        def slot(zz, xx):
            return wg.at[zz, pl.ds(pl.multiple_of(xx * shard + h * piece_rows, piece_rows), piece_rows), :]

        return slot

    w_slots = [w_slot_of(h) for h in range(parts)]
    half_rows = rows // 2

    def x_half(member, h):
        return xg.at[member, pl.ds(h * half_rows, half_rows), :]

    def o_slot(zz, xx):
        return wog.at[core, pl.ds(pl.multiple_of(dp_at(zz, xx) * shard, shard), shard), :]

    lo = jnp.minimum(z, nz - 1 - z)

    def piece(i):
        near = z - (i + 1) // 2 if i % 2 else z + (i + 1) // 2
        far = jnp.where(z > nz - 1 - z, z - (i - lo), z + (i - lo))
        return jnp.where(i <= 2 * lo, near, far) if i else z

    def first_hops(slot, ss, rs):
        left = remote(slot(z, x), slot(z, x), ss.at[nz], rs.at[z], dp_at(jnp.maximum(z - 1, 0), x), me)
        right = remote(
            slot(z, x), slot(z, x), ss.at[nz + 1], rs.at[z], dp_at(jnp.minimum(z + 1, nz - 1), x), me
        )
        return left, right

    def next_hops(slot, ss, rs, i):
        p = piece(i)
        left = remote(slot(p, x), slot(p, x), ss.at[p], rs.at[p], dp_at(jnp.maximum(z - 1, 0), x), me)
        right = remote(
            slot(p, x), slot(p, x), ss.at[p], rs.at[p], dp_at(jnp.minimum(z + 1, nz - 1), x), me
        )
        return left, right

    line_sends = []

    def line_start(slot, ss, rs, i):
        if nz == 1:
            return
        p = piece(i)
        left, right = next_hops(slot, ss, rs, i) if i else first_hops(slot, ss, rs)
        to_left = jnp.logical_and(p >= z, z > 0)
        to_right = jnp.logical_and(p <= z, z < nz - 1)
        line_sends.append((to_left, left))
        line_sends.append((to_right, right))

        @pl.when(to_left)
        def _():
            left.start()

        @pl.when(to_right)
        def _():
            right.start()

    def across(slot, ss, rs, i):
        p = piece(i)
        for k in range(1, nx):
            go(remote(slot(p, x), slot(p, x), ss.at[p, k], rs.at[p, k], dp_at(z, (x + k) % nx), me))

    def shared(p, xx, k):
        idx = dp_at(p, xx)
        slot = o_slot(p, xx)
        return remote(slot, slot, oc_s.at[idx, k], oc_r.at[idx, k], dp, seq_at(y, (core + k) % nc))

    def share(p, xx):
        for k in range(1, nc):
            shared(p, xx, k).start()

    def w_relay(i):
        p = piece(i)
        for h, slot in enumerate(w_slots):
            arrive(slot(p, x), wz_r.at[h, p])
            line_start(slot, wz_s.at[h], wz_r.at[h], i)
            across(slot, wx_s.at[h], wx_r.at[h], i)

    def o_relay(i):
        p = piece(i)
        arrive(o_slot(p, x), oz_r.at[p])
        line_start(o_slot, oz_s, oz_r, i)
        across(o_slot, ox_s, ox_r, i)
        share(p, x)

    def o_crossed(i):
        p = piece(i)
        for k in range(1, nx):
            xx = (x - k + nx) % nx
            arrive(o_slot(p, xx), ox_r.at[p, k])
            share(p, xx)

    own = []
    for part in range(3):
        own.append(
            pltpu.make_async_copy(
                w_ref.at[:, pl.ds(pl.multiple_of(part * width + me * cols, 128), cols)],
                wg.at[
                    z,
                    pl.ds(pl.multiple_of(x * shard, shard), shard),
                    pl.ds(part * cols, cols),
                ],
                local_sem.at[part],
            )
        )
    own.append(pltpu.make_async_copy(x_ref, xg.at[me], local_sem.at[3]))
    own.append(pltpu.make_async_copy(ids_ref, idg.at[me], local_sem.at[4]))
    own.append(
        pltpu.make_async_copy(
            wo_ref.at[:, pl.ds(pl.multiple_of(core * (width // nc), 128), width // nc)],
            o_slot(z, x),
            local_sem.at[5],
        )
    )
    for c in own:
        c.start()

    barrier = pltpu.get_barrier_semaphore()

    def greet_seq(i, _):
        pl.semaphore_signal(
            barrier, inc=1, device_id=(dp, (me + i) % n), device_id_type=MESH
        )
        return 0

    def greet_dp(i, _):
        pl.semaphore_signal(
            barrier, inc=1, device_id=((dp + i) % ndp, me), device_id_type=MESH
        )
        return 0

    lax.fori_loop(1, n, greet_seq, 0)
    lax.fori_loop(1, ndp, greet_dp, 0)
    pl.semaphore_wait(barrier, n - 1 + ndp - 1)

    own[0].wait()
    own[1].wait()
    own[2].wait()
    for h, slot in enumerate(w_slots):
        line_start(slot, wz_s.at[h], wz_r.at[h], 0)
        across(slot, wx_s.at[h], wx_r.at[h], 0)
    own[4].wait()
    for i in range(1, n):
        go(remote(idg.at[me], idg.at[me], id_s.at[i], id_r.at[i], dp, (me + i) % n))
    own[3].wait()
    for h in range(2):
        for i in range(1, ny):
            own_half = x_half(me, h)
            go(remote(own_half, own_half, xy_s.at[h, i], xy_r.at[h, i], dp, seq_at((y + i) % ny, core)))
    for k in range(1, nc):
        go(remote(xg.at[me], xg.at[me], xc_s.at[0, 0, k], xc_r.at[0, 0, k], dp, seq_at(y, (core + k) % nc)))
    own[5].wait()
    line_start(o_slot, oz_s, oz_r, 0)
    across(o_slot, ox_s, ox_r, 0)
    share(z, x)

    gain = gain_ref[...]

    def norm_rows(member, h):
        base = pl.multiple_of(member * rows, rows)

        def body(b, _):
            r0 = pl.multiple_of(h * half_rows + b * 64, 64)
            wide = xg[member, pl.ds(r0, 64), :].astype(jnp.float32)
            ms = jnp.mean(wide * wide, axis=-1, keepdims=True)
            out = (wide * lax.rsqrt(ms + EPS) * gain).astype(jnp.bfloat16)
            for g in range(nz):
                normed[g, pl.ds(base + r0, 64), :] = out[:, g * chunk : (g + 1) * chunk]
            return 0

        lax.fori_loop(0, half_rows // 64, body, 0)

    def x_relay(h):
        for i in range(1, ny):
            source = seq_at((y - i + ny) % ny, core)
            slot = x_half(source, h)
            arrive(slot, xy_r.at[h, i])
            for k in range(1, nc):
                go(remote(slot, slot, xc_s.at[h, i, k], xc_r.at[h, i, k], dp, seq_at(y, (core + k) % nc)))
            norm_rows(source, h)

    def x_shared(h):
        for i in range(1, ny):
            for k in range(1, nc):
                other = seq_at((y - i + ny) % ny, (core - k + nc) % nc)
                arrive(x_half(other, h), xc_r.at[h, i, k])
                norm_rows(other, h)

    for h in range(2):
        norm_rows(me, h)
    for k in range(1, nc):
        other = seq_at(y, (core - k + nc) % nc)
        arrive(xg.at[other], xc_r.at[0, 0, k])
        for h in range(2):
            norm_rows(other, h)
    for i in range(1, nz):
        w_relay(i)
        if i == 1:
            x_relay(0)
    if nz == 1:
        x_relay(0)
    x_relay(1)
    for h in range(2):
        x_shared(h)

    for i in range(1, n):
        arrive(idg.at[(me - i + n) % n], id_r.at[i])
    for m in range(n):
        line = jnp.broadcast_to(idg[m].astype(jnp.float32), (128, rows))
        idcol[pl.ds(m * rows, rows), :] = jnp.transpose(line)
    id_row = jnp.concatenate([idg[m] for m in range(n)], axis=1).astype(jnp.float32)

    row_block = 256
    blocks = seq_len // row_block

    def project(i, first):
        zz = piece(i)
        for k in range(1, nx):
            for h, slot in enumerate(w_slots):
                arrive(slot(zz, (x - k + nx) % nx), wx_r.at[h, zz, k])

        def body(b, _):
            r = pl.ds(pl.multiple_of(b * row_block, row_block), row_block)
            prod = jnp.dot(normed[zz, r, :], wg[zz], preferred_element_type=jnp.float32)
            if first:
                acc[r, :] = prod
            else:
                acc[r, :] = acc[r, :] + prod
            return 0

        lax.fori_loop(0, blocks, body, 0)

    for i in range(nz):
        if i == max(0, nz - 2):
            for e in range(1, nz - 2):
                o_relay(e)
        project(i, i == 0)
    if nz > 2:
        o_relay(nz - 2)

    def group_of(shape, dim):
        return lax.div(lax.broadcasted_iota(jnp.int32, shape, dim), jnp.int32(channel))

    same_head = (group_of((cols, cols), 0) == group_of((cols, cols), 1)).astype(jnp.float32)
    same_head = same_head.astype(jnp.bfloat16)
    scale_row = jnp.zeros((1, cols), jnp.float32)
    for h in range(heads):
        scale_row = jnp.where(group_of((1, cols), 1) == h, scale_ref[me * heads + h], scale_row)
    scale_row = scale_row / math.sqrt(channel)

    def head_scale(values):
        square = values * values
        high = square.astype(jnp.bfloat16)
        low = (square - high.astype(jnp.float32)).astype(jnp.bfloat16)
        total = jnp.dot(high, same_head, preferred_element_type=jnp.float32) + jnp.dot(
            low, same_head, preferred_element_type=jnp.float32
        )
        return lax.rsqrt(total / channel + EPS)

    def split(b, _):
        r = pl.ds(pl.multiple_of(b * row_block, row_block), row_block)
        joined = acc[r, :].astype(jnp.bfloat16)
        q = joined[:, :cols].astype(jnp.float32)
        k = joined[:, cols : 2 * cols].astype(jnp.float32)
        qs[r, :] = (q * head_scale(q) * scale_row).astype(jnp.bfloat16)
        ks[r, :] = (k * head_scale(k)).astype(jnp.bfloat16)
        vs[r, :] = joined[:, 2 * cols :]
        return 0

    lax.fori_loop(0, blocks, split, 0)

    if nz > 1:
        o_relay(nz - 1)
    o_crossed(0)

    q_block = cfg["q_block"]
    lane_head = group_of((q_block, cols), 1)

    def stage_target(t, sign):
        dy = (t // nc + 1) % ny
        dc = (t + 1) % nc
        if sign > 0:
            return seq_at((y + dy) % ny, (core + dc) % nc)
        return seq_at((y - dy + ny) % ny, (core - dc + nc) % nc)

    def a2a(t):
        j = stage_target(t, 1)
        return remote(ao.at[j], ag.at[me], at_s.at[t], at_r.at[t], dp, j)

    def stage(t, _):
        j = stage_target(t, 1)
        for sub in range(rows // q_block):
            r = pl.ds(pl.multiple_of(j * rows + sub * q_block, q_block), q_block)
            bias = jnp.where(idcol[r, :][:, :1] == id_row, 0.0, NEG)
            qb = qs[r, :]
            out = jnp.zeros((q_block, cols), jnp.float32)
            for h in range(heads):
                mine = lane_head == h
                qh = jnp.where(mine, qb, jnp.zeros_like(qb))
                s = lax.dot_general(
                    qh, ks[...], (((1,), (1,)), ((), ())), preferred_element_type=jnp.float32
                )
                s = s + bias
                p = jnp.exp(s - jnp.max(s, axis=-1, keepdims=True))
                total = jnp.sum(p, axis=-1, keepdims=True)
                o = jnp.dot(p.astype(jnp.bfloat16), vs[...], preferred_element_type=jnp.float32)
                out = jnp.where(mine, o / total, out)
            ao[j, pl.ds(sub * q_block, q_block), :] = out.astype(jnp.bfloat16)

        @pl.when(t < n - 1)
        def _():
            a2a(t).start()

        for i in range(1, nz):

            @pl.when(t == min(i - 1, n - 1))
            def _(i=i):
                o_crossed(i)

        return 0

    lax.fori_loop(0, n, stage, 0)

    for t in range(n - 1):
        arrive(ag.at[stage_target(t, -1)], at_r.at[t])
    ag[me] = ao[me]

    attention = jnp.concatenate([ag[m] for m in range(n)], axis=1)
    for k in range(nc):
        g = (core - k + nc) % nc
        if k:
            half = wog.at[g]
            for d in range(ndp):
                arrive(half.at[pl.ds(d * shard, shard), :], oc_r.at[d, k])
        lanes = pl.ds(pl.multiple_of(g * (width // nc), 128), width // nc)
        prod = jnp.dot(attention, wog[g], preferred_element_type=jnp.float32)
        mixed_ref[:, lanes] = (xg[me, :, lanes].astype(jnp.float32) + prod).astype(jnp.bfloat16)

    logits = lax.dot_general(
        bits_ref[...], mixed_ref[...], (((1,), (1,)), ((), ())), preferred_element_type=jnp.float32
    )
    eye = lax.broadcasted_iota(jnp.int32, (bits, bits), 0) == lax.broadcasted_iota(
        jnp.int32, (bits, bits), 1
    )
    offset = jnp.sum(jnp.where(eye, off_ref[...], 0.0), axis=1, keepdims=True)
    probs = jax.nn.sigmoid(4.0 * (logits + offset))
    lanes_eye = lax.broadcasted_iota(jnp.int32, (bits, 128), 0) == lax.broadcasted_iota(
        jnp.int32, (bits, 128), 1
    )
    own_sums = jnp.sum(probs, axis=1, keepdims=True)
    part1[me, :, :] = jnp.sum(jnp.where(lanes_eye, own_sums, 0.0), axis=0, keepdims=True)
    for i in range(1, n):
        go(remote(part1.at[me], part1.at[me], p1_s.at[i], p1_r.at[i], dp, (me + i) % n))
    for i in range(1, n):
        arrive(part1.at[(me - i + n) % n], p1_r.at[i])
    pack = part1[0]
    for m in range(1, n):
        pack = pack + part1[m]
    part2[dp, :, :] = pack
    for i in range(1, ndp):
        go(remote(part2.at[dp], part2.at[dp], p2_s.at[i], p2_r.at[i], (dp + i) % ndp, me))
    for i in range(1, ndp):
        arrive(part2.at[(dp - i + ndp) % ndp], p2_r.at[i])
    total = part2[0]
    for m in range(1, ndp):
        total = total + part2[m]
    marginal = total / (seq_len * ndp)
    line = marginal[:, :bits]
    ent_ref[...] = -(line * jnp.log(line) + (1.0 - line) * jnp.log(1.0 - line))
    codes = probs - jnp.sum(jnp.where(lanes_eye, marginal, 0.0), axis=1, keepdims=True)
    for b in range(bits):
        codes_ref[b] = codes[b : b + 1, :]

    for c in sends:
        c.wait_send()
    for t in range(n - 1):
        a2a(t).wait_send()
    for d in range(ndp):
        for k in range(1, nc):
            shared(d // nx, d % nx, k).wait_send()
    for cond, c in line_sends:

        @pl.when(cond)
        def _(c=c):
            c.wait_send()


def on_device(
    cfg,
    residual_tiles,
    picture_label_tile,
    prenorm_multiplier,
    triple_projector,
    logit_scaling,
    final_projector,
    binarizer_projector,
    binarizer_offset,
):
    nz, nx, ny, nc = cfg["nz"], cfg["nx"], cfg["ny"], cfg["nc"]
    n, ndp = ny * nc, nz * nx
    _, rows, width = residual_tiles.shape
    heads_all = logit_scaling.shape[0]
    bits = binarizer_projector.shape[1]
    cols = width // n
    shard = triple_projector.shape[0]
    seq_len = rows * n
    parts = 2 if shard % 32 == 0 else 1
    cfg = dict(cfg, heads=heads_all // n, channel=width // heads_all, q_block=min(256, rows), parts=parts)
    dma = pltpu.SemaphoreType.DMA
    vmem, hbm = pl.BlockSpec(memory_space=pltpu.VMEM), pl.BlockSpec(memory_space=pl.ANY)
    smem = pl.BlockSpec(memory_space=pltpu.SMEM)
    bf16, f32 = jnp.bfloat16, jnp.float32
    mixed, codes, ent = pl.pallas_call(
        functools.partial(layer_kernel, cfg),
        out_shape=(
            jax.ShapeDtypeStruct((rows, width), bf16),
            jax.ShapeDtypeStruct((bits, 1, rows), f32),
            jax.ShapeDtypeStruct((1, bits), f32),
        ),
        in_specs=[hbm, vmem, vmem, hbm, smem, hbm, vmem, vmem],
        out_specs=(vmem, vmem, vmem),
        scratch_shapes=[
            pltpu.VMEM((nz, nx * shard, 3 * cols), bf16),
            pltpu.VMEM((nc, width, width // nc), bf16),
            pltpu.VMEM((n, rows, width), bf16),
            pltpu.VMEM((n, 1, rows), jnp.int32),
            pltpu.VMEM((seq_len, 128), f32),
            pltpu.VMEM((nz, seq_len, nx * shard), bf16),
            pltpu.VMEM((seq_len, 3 * cols), f32),
            pltpu.VMEM((seq_len, cols), bf16),
            pltpu.VMEM((seq_len, cols), bf16),
            pltpu.VMEM((seq_len, cols), bf16),
            pltpu.VMEM((n, rows, cols), bf16),
            pltpu.VMEM((n, rows, cols), bf16),
            pltpu.VMEM((n, 1, 128), f32),
            pltpu.VMEM((ndp, 1, 128), f32),
            dma((6,)),
            dma((parts, nz + 2)),
            dma((parts, nz)),
            dma((parts, nz, nx)),
            dma((parts, nz, nx)),
            dma((nz + 2,)),
            dma((nz,)),
            dma((nz, nx)),
            dma((nz, nx)),
            dma((ndp, nc)),
            dma((ndp, nc)),
            dma((2, ny)),
            dma((2, ny)),
            dma((2, ny, nc)),
            dma((2, ny, nc)),
            dma((n,)),
            dma((n,)),
            dma((n,)),
            dma((n,)),
            dma((n,)),
            dma((n,)),
            dma((ndp,)),
            dma((ndp,)),
        ],
        compiler_params=pltpu.CompilerParams(
            collective_id=0, has_side_effects=True, vmem_limit_bytes=60 * 1024 * 1024
        ),
        name="layer",
    )(
        residual_tiles[0],
        picture_label_tile,
        prenorm_multiplier[None],
        triple_projector,
        logit_scaling,
        final_projector,
        binarizer_projector.T,
        binarizer_offset[None],
    )
    return mixed[None], jnp.swapaxes(codes, 0, 1), ent[0]


def solution(mesh):
    ndp, n = mesh.shape["dp"], mesh.shape["seq"]
    nx = math.isqrt(ndp // 2)
    if nx < 1 or ndp % nx:
        nx = 1
    nc = 2 if n % 2 == 0 else 1
    cfg = {"nz": ndp // nx, "nx": nx, "ny": n // nc, "nc": nc}
    return jax.shard_map(
        functools.partial(on_device, cfg),
        mesh=mesh,
        in_specs=(
            P("dp", "seq", None),
            P("dp", "seq"),
            P(),
            P("dp", None),
            P(),
            P("dp", None),
            P(),
            P(),
        ),
        out_specs=(P("dp", "seq", None), P("dp", None, "seq"), P()),
        check_vma=False,
    )
```
